32 devices in a mesh: seg: 4 (over y, x), sec: 8 (over z, core).
Axes of the slice: x: 2, y: 2, z: 4, core: 2. Of those that a mesh axis runs over, the one named last changes fastest.
Arguments:
- left_env: bfloat16 [4, 8, 13, 512, 512], P('seg', 'sec'), may hold values from -0.25 to 0.25
- right_env: bfloat16 [4, 8, 13, 512, 512], P('seg', 'sec'), may hold values from -0.25 to 0.25
- left_block: bfloat16 [4, 8, 512, 512], P('seg', 'sec'), may hold values from -8 to 8
- right_block: bfloat16 [4, 8, 512, 512], P('seg', 'sec'), may hold values from -0.25 to 0.25
- inv_sv: bfloat16 [4, 8, 512], P('seg', 'sec'), may hold values from 0.5 to 2
- precond: float32 [4, 8, 512, 512], P('seg', 'sec'), may hold values from 1 to 4
- sector_dims: int32 [4, 8, 2], P('seg', 'sec'), may hold values from 128 to 512, as said below
- channel_charge: int32 [13], replicated, may hold values from -1 to 1
Outputs:
- next_vector: bfloat16 [4, 8, 512, 512], P('seg', 'sec')
- last_image: float32 [4, 8, 512, 512], P('seg', 'sec')
- projected: float32 [4, 4, 4], P('seg')
The draws below stay inside these ranges and needn't reach their ends.
Inputs may be any that keep to these rules, and one draw needn't show every extreme that they name: `sector_dims`: in every segment some sector has left bond dimension 512 and some sector has right bond dimension 512.
All inputs are finite; a program needn't handle non-finite values.
Results may differ from the reference program's by a relative error of at most 0.024.
Values may be sent and summed in bfloat16 or wider, within the bound.
A program may use at most 64 MiB of HBM per device.

```python
import math
import jax
import jax.numpy as jnp
from jax import lax

M = 512
W = 13
MATVECS = 4
SEGS = 4
SECTORS = 8


def draw_sector_dims(key, part):
    first_key, second_key = jax.random.split(jax.random.fold_in(key, 7))
    dims = jax.random.randint(first_key, (SEGS, SECTORS, 2), M // 4, M + 1)
    picked = jax.random.randint(second_key, (SEGS, 2), 0, SECTORS)
    hit = jnp.arange(SECTORS)[None, :, None] == picked[:, None, :]
    return jnp.where(hit, M, dims).astype(jnp.int32)


def draw_left_block(key, part):
    inner_key = jax.random.fold_in(key, 11)
    position = jnp.arange(SECTORS, dtype=jnp.float32) / max(SECTORS - 1, 1)
    factor = jnp.exp(jnp.log(0.4) + position * jnp.log(5.0))
    values = jax.random.normal(inner_key, (SEGS, SECTORS, M, M), jnp.float32)
    return jnp.clip(values * factor[None, :, None, None], -8.0, 8.0).astype(jnp.bfloat16)


def plant(drawn, stream_key, low, high):
    longest = drawn.shape.index(max(drawn.shape))
    spots = []
    for shift in (0, 1):
        where = [jax.random.randint(jax.random.fold_in(stream_key, axis), (), 0, length) for axis, length in enumerate(drawn.shape)]
        where[longest] = (where[longest] + shift) % drawn.shape[longest]
        spots.append(tuple(where))
    return drawn.at[spots[0]].set(low).at[spots[1]].set(high)


def steps_of(stream_key, shape, cuts, low, largest):
    def one(axis_at, shards_of):
        steps = jax.random.uniform(jax.random.fold_in(jax.random.fold_in(stream_key, 6), axis_at), (shards_of,), jnp.float32, low / len(cuts), largest / len(cuts))
        return jnp.repeat(jnp.exp(steps), shape[axis_at] // shards_of).reshape((-1,) + (1,) * (len(shape) - axis_at - 1))

    gain = one(*cuts[0])
    for cut in cuts[1:]:
        gain = gain * one(*cut)
    return gain


def gaussian(stream_key, shape, width, bound, cuts=(), kind=jnp.bfloat16):
    values = width * jax.random.normal(stream_key, shape, jnp.float32)
    if cuts:
        values = values * steps_of(stream_key, shape, cuts, -0.22, 0.18)
    return jnp.clip(values, -bound, bound).astype(kind)


def setup_inputs(seed: int = 0) -> dict:
    splits = jax.random.split(jax.random.key(seed), 9)
    return {
        "left_env": gaussian(splits[0], (SEGS, SECTORS, W, M, M), M ** -0.5, 0.25, ((0, 4), (1, 8))),
        "right_env": gaussian(splits[1], (SEGS, SECTORS, W, M, M), M ** -0.5, 0.25, ((0, 4), (1, 8))),
        "left_block": draw_left_block(jax.random.fold_in(splits[8], 71), 0),
        "right_block": gaussian(splits[3], (SEGS, SECTORS, M, M), M ** -0.5, 0.25, ((0, 4), (1, 8))),
        "inv_sv": jnp.clip(jnp.exp(math.log(2.0) - 1.3862944 * jax.random.uniform(splits[4], (SEGS, SECTORS, M), jnp.float32) ** steps_of(splits[4], (SEGS, SECTORS, M), ((0, 4), (1, 8)), -0.2, 0.2)), 0.5, 2.0).astype(jnp.bfloat16),
        "precond": jnp.clip(jnp.exp(math.log(4.0) - 1.3862944 * jax.random.uniform(splits[5], (SEGS, SECTORS, M, M), jnp.float32) ** steps_of(splits[5], (SEGS, SECTORS, M, M), ((0, 4), (1, 8)), -0.2, 0.2)), 1.0, 4.0),
        "sector_dims": draw_sector_dims(jax.random.fold_in(splits[8], 71), 0),
        "channel_charge": plant(jax.random.randint(splits[7], (W,), -1, 2), jax.random.fold_in(splits[7], 1), -1, 1).astype(jnp.int32),
    }


def reference(left_env, right_env, left_block, right_block, inv_sv, precond, sector_dims, channel_charge):
    eps = 1e-06
    index = jnp.arange(M, dtype=jnp.int32)
    mask = ((index[None, None, :, None] < sector_dims[:, :, 0, None, None]) & (index[None, None, None, :] < sector_dims[:, :, 1, None, None])).astype(jnp.float32)
    count = SECTORS * M * M

    def inner(first, second):
        return lax.optimization_barrier(jnp.sum(first * second, axis=(1, 2, 3))) / count

    def expand(value):
        return value[:, None, None, None]
    neighbour_block = jnp.roll(right_block, -1, axis=0)
    neighbour_inv = jnp.roll(inv_sv, -1, axis=0)
    scaled = (left_block.astype(jnp.float32) * neighbour_inv.astype(jnp.float32)[:, :, None, :]).astype(jnp.bfloat16)
    guess = jnp.einsum('gsab,gsbc->gsac', scaled.astype(jnp.float32), neighbour_block.astype(jnp.float32)) * mask
    first = (guess * expand(lax.rsqrt(inner(guess, guess) + eps))).astype(jnp.bfloat16)
    select = (channel_charge[:, None] == jnp.array([-1, 0, 1], dtype=jnp.int32)[None, :]).astype(jnp.float32)
    left_flat = left_env.reshape(SEGS * SECTORS, W, M, M)
    right_flat = right_env.reshape(SEGS * SECTORS, W, M, M)

    def apply(vector):
        vector_flat = vector.reshape(SEGS * SECTORS, M, M)

        def single(pieces):
            left_one, right_one, vec_one = pieces
            left_x = jnp.einsum('wab,bc->wac', left_one.astype(jnp.float32), vec_one.astype(jnp.float32)).astype(jnp.bfloat16)
            terms = jnp.einsum('wac,wdc->wad', left_x.astype(jnp.float32), right_one.astype(jnp.float32))
            return jnp.stack([lax.optimization_barrier(jnp.sum(terms * select[:, q, None, None], axis=0)) for q in range(3)])
        grouped = lax.map(single, (left_flat, right_flat, vector_flat)).reshape(SEGS, SECTORS, 3, M, M)
        to_lower = grouped[:, :, 0]
        stay = grouped[:, :, 1]
        to_upper = grouped[:, :, 2]
        zero = jnp.zeros_like(stay[:, :1])
        from_lower = jnp.concatenate([zero, to_upper[:, :-1]], axis=1)
        from_upper = jnp.concatenate([to_lower[:, 1:], zero], axis=1)
        return (stay + from_lower + from_upper) * mask
    basis = [first]
    columns = []
    image = None
    for step in range(MATVECS):
        current = basis[step]
        image = apply(current)
        column = [inner(basis[j].astype(jnp.float32), image) for j in range(step + 1)]
        column = column + [jnp.zeros((SEGS,), jnp.float32) for j in range(MATVECS - step - 1)]
        columns.append(jnp.stack(column, axis=1))
        theta = column[step]
        resid = image - expand(theta) * current.astype(jnp.float32)
        correction = resid / precond
        projected_part = jnp.zeros_like(correction)
        for j in range(step + 1):
            weight = inner(basis[j].astype(jnp.float32), correction)
            projected_part = projected_part + expand(weight) * basis[j].astype(jnp.float32)
        remain = correction - projected_part
        basis.append((remain * expand(lax.rsqrt(inner(remain, remain) + eps))).astype(jnp.bfloat16))
    projected = jnp.stack(columns, axis=2)
    return (basis[-1], image, projected)
```

```python
import functools

import jax
import jax.numpy as jnp
from jax import lax
from jax.experimental import pallas as pl
from jax.experimental.pallas import tpu as pltpu
from jax.sharding import PartitionSpec as P

MATVECS = 4
EPS = 1e-06
ROWS = 256
COLS = 256
CHUNK = 32
MESH = pl.DeviceIdType.MESH


def fold(values):
    rows, columns = values.shape
    block = jnp.sum(values.reshape(rows // 8, 8, columns), axis=0)
    total = block[:, :128]
    for at in range(128, columns, 128):
        total = total + block[:, at : at + 128]
    return total


def spread(tile, rows, columns):
    wide = jnp.concatenate([tile] * (columns // 128), axis=1)
    return jnp.concatenate([wide] * (rows // 8), axis=0)


def kernel(
    segs, secs,
    charge_ref, dims_ref, left_hbm, right_hbm, block_hbm, other_hbm, inv_ref, precond_hbm,
    next_hbm, image_hbm, projected_ref,
    left_ref, right_ref, block_ref, pinv_ref, nb_ref, ninv_ref, scaled_ref, basis_ref,
    up_basis, low_basis, up_pinv, low_pinv, lx_ref, prefix_ref,
    stay_ref, up_out, low_out, up_in, low_in, image_ref, remain_ref, following_ref,
    slots_ref, norm_ref, scale_ref, proj_ref, order_ref,
    load_sem, guess_send, guess_recv, pinv_send, pinv_recv, halo_send, halo_recv,
    edge_send, edge_recv, sum_send, sum_recv, store_sem,
):
    channels, width, _ = left_ref.shape
    tiles = width // ROWS
    halves = width // COLS
    pieces = tiles * halves
    edge = width - ROWS
    count = secs * width * width
    f32, bf16 = jnp.float32, jnp.bfloat16
    seg, sec = lax.axis_index("seg"), lax.axis_index("sec")
    seg_before = lax.rem(seg + segs - 1, segs)
    seg_after = lax.rem(seg + 1, segs)
    above = (seg, lax.rem(sec + 1, secs))
    below = (seg, lax.rem(sec + secs - 1, secs))
    has_above = sec < secs - 1
    has_below = sec > 0
    edge_rows = pl.ds(edge, ROWS)

    load_left = pltpu.make_async_copy(left_hbm, left_ref, load_sem.at[0])
    load_right = pltpu.make_async_copy(right_hbm, right_ref, load_sem.at[1])
    load_block = pltpu.make_async_copy(block_hbm, block_ref, load_sem.at[2])
    load_precond = pltpu.make_async_copy(precond_hbm, pinv_ref, load_sem.at[3])
    load_precond.start()
    load_block.start()
    load_left.start()
    load_right.start()

    barrier = pltpu.get_barrier_semaphore()
    pl.semaphore_signal(barrier, inc=1, device_id=(seg_before, sec), device_id_type=MESH)
    pl.semaphore_signal(barrier, inc=1, device_id=(seg_after, sec), device_id_type=MESH)
    for offset in range(1, secs):
        peer = lax.rem(sec + offset, secs)
        pl.semaphore_signal(barrier, inc=1, device_id=(seg, peer), device_id_type=MESH)
    pl.semaphore_wait(barrier, secs + 1)

    def remote(src, dst, send, recv, device):
        return pltpu.make_async_remote_copy(
            src_ref=src, dst_ref=dst, send_sem=send, recv_sem=recv,
            device_id=device, device_id_type=MESH,
        )

    send_inv = remote(
        inv_ref, ninv_ref, guess_send.at[0], guess_recv.at[0], (seg_before, sec)
    )

    def send_block(h):
        across = pl.ds(h * COLS, COLS)
        return remote(
            other_hbm.at[:, across], nb_ref.at[:, across],
            guess_send.at[h + 1], guess_recv.at[h + 1], (seg_before, sec),
        )

    send_inv.start()
    for h in range(halves):
        send_block(h).start()

    to_above = remote(
        precond_hbm.at[edge_rows, :], low_pinv, pinv_send.at[0], pinv_recv.at[0], above
    )
    to_below = remote(
        precond_hbm.at[edge_rows, :], up_pinv, pinv_send.at[1], pinv_recv.at[1], below
    )

    def basis_above(k):
        return remote(
            basis_ref.at[k, edge_rows, :], low_basis.at[k],
            edge_send.at[0, k], edge_recv.at[0, k], above,
        )

    def basis_below(k):
        return remote(
            basis_ref.at[k, edge_rows, :], up_basis.at[k],
            edge_send.at[1, k], edge_recv.at[1, k], below,
        )

    def up_copy(n):
        return remote(
            up_out.at[n], up_in.at[n], halo_send.at[0, n], halo_recv.at[0, n], above
        )

    def low_copy(n):
        return remote(
            low_out.at[n], low_in.at[n], halo_send.at[1, n], halo_recv.at[1, n], below
        )

    pl.when(has_above)(lambda: to_above.start())
    pl.when(has_below)(lambda: to_below.start())

    keys = []
    for w in range(channels):
        q = charge_ref[w]
        keys.append(jnp.where(q == 1, 0, jnp.where(q == -1, 1, 2)))
    raising = jnp.int32(0)
    moving = jnp.int32(0)
    for w in range(channels):
        raising = raising + jnp.where(keys[w] == 0, 1, 0)
        moving = moving + jnp.where(keys[w] <= 1, 1, 0)
    places = []
    for w in range(channels):
        place = jnp.int32(0)
        for v in range(channels):
            if v < w:
                place = place + jnp.where(keys[v] <= keys[w], 1, 0)
            elif v > w:
                place = place + jnp.where(keys[v] < keys[w], 1, 0)
        places.append(place)
    for i in range(channels):
        who = jnp.int32(0)
        for w in range(channels):
            who = who + jnp.where(places[w] == i, w, 0)
        order_ref[i] = who

    proj_ref[...] = jnp.zeros_like(proj_ref)

    def chunked(rows, body):
        @pl.loop(0, rows // CHUNK)
        def _(c):
            body(pl.ds(pl.multiple_of(c * CHUNK, CHUNK), CHUNK))

    def clear(at):
        for k in range(1, MATVECS):
            basis_ref[k, at, :] = jnp.zeros((CHUNK, width), bf16)

    def clear_prefix(at):
        prefix_ref[0, at, :] = jnp.zeros((CHUNK, COLS), f32)

    chunked(width, clear)
    chunked(ROWS, clear_prefix)

    def no_neighbour(halo, vectors, inverse):
        @pl.loop(0, MATVECS * pieces)
        def _(n):
            halo[n] = jnp.zeros((ROWS, COLS), bf16)

        @pl.loop(0, MATVECS)
        def _(k):
            vectors[k] = jnp.zeros((ROWS, width), bf16)

        inverse[...] = jnp.ones((ROWS, width), f32)

    pl.when(sec == 0)(lambda: no_neighbour(up_in, low_basis, low_pinv))
    pl.when(sec == secs - 1)(lambda: no_neighbour(low_in, up_basis, up_pinv))

    def invert(ref):
        def body(at):
            ref[at, :] = 1.0 / ref[at, :]

        chunked(ref.shape[0], body)

    load_precond.wait()
    invert(pinv_ref)

    def masked(values, start, left=0):
        row = start + lax.broadcasted_iota(jnp.int32, values.shape, 0)
        column = left + lax.broadcasted_iota(jnp.int32, values.shape, 1)
        inside = (row < dims_ref[0]) & (column < dims_ref[1])
        return jnp.where(inside, values, 0.0)

    lane = lax.broadcasted_iota(jnp.int32, (8, 128), 1)
    line = lax.broadcasted_iota(jnp.int32, (8, 128), 0)
    zero = jnp.zeros((8, 128), f32)

    def sum_copies(r):
        own = slots_ref.at[r, sec]
        return [
            remote(
                own, own, sum_send.at[r], sum_recv.at[r],
                (seg, lax.rem(sec + offset, secs)),
            )
            for offset in range(1, secs)
        ]

    def publish(r, parts):
        tile = zero
        for at, part in parts.items():
            tile = jnp.where(lane == at, jnp.sum(part, axis=1, keepdims=True), tile)
        slots_ref[r, sec] = jnp.sum(tile, axis=0, keepdims=True)
        for copy in sum_copies(r):
            copy.start()

    def collect(r):
        arrived = slots_ref.at[r, pl.ds(0, secs - 1)]
        pltpu.make_async_copy(arrived, arrived, sum_recv.at[r]).wait()
        total = jnp.sum(slots_ref[r], axis=0) * (1.0 / count)
        total = jnp.broadcast_to(total, (8, 128))

        def entry(at):
            value = jnp.sum(jnp.where(lane == at, total, 0.0), axis=1, keepdims=True)
            return jnp.broadcast_to(value, (8, 128))

        return entry

    def left_part(k, t, h):
        rows, across = pl.ds(t * ROWS, ROWS), pl.ds(h * COLS, COLS)
        vector = basis_ref[k, :, across]
        for w in range(channels):
            lx_ref[w, rows, across] = jnp.dot(
                left_ref[w, rows, :], vector, preferred_element_type=f32
            ).astype(bf16)

    send_inv.wait_recv()
    load_block.wait()
    scaled_ref[...] = (
        block_ref[...].astype(f32) * ninv_ref[...].astype(f32)
    ).astype(bf16)

    guess_sq = zero
    for h in range(halves):
        across = pl.ds(h * COLS, COLS)
        send_block(h).wait_recv()
        for t in range(tiles):
            rows = pl.ds(t * ROWS, ROWS)
            guess = masked(
                jnp.dot(
                    scaled_ref[rows, :], nb_ref[:, across], preferred_element_type=f32
                ),
                t * ROWS, h * COLS,
            )
            basis_ref[0, rows, across] = guess.astype(bf16)
            guess_sq = guess_sq + fold(guess * guess)
        if h == 0:
            load_left.wait()
        if h < halves - 1:
            for t in range(tiles):
                left_part(0, t, h)
        if h == 0:
            @pl.when(has_below)
            def _():
                to_above.wait_recv()

            @pl.when(has_above)
            def _():
                to_below.wait_recv()

            invert(up_pinv)
            invert(low_pinv)
            load_right.wait()
    norm_ref[...] = guess_sq
    pl.when(has_above)(lambda: basis_above(0).start())
    pl.when(has_below)(lambda: basis_below(0).start())

    @pl.loop(0, MATVECS)
    def _(k):
        def gather(piece):
            n = k * pieces + piece

            @pl.when(has_below)
            def _():
                up_copy(n).wait_recv()

            @pl.when(has_above)
            def _():
                low_copy(n).wait_recv()

        def arrived(piece, c):
            t, h = divmod(piece, halves)
            n = k * pieces + piece
            across = pl.ds(h * COLS, COLS)
            inner = pl.ds(pl.multiple_of(c * CHUNK, CHUNK), CHUNK)
            start = t * ROWS + c * CHUNK
            at = pl.ds(pl.multiple_of(start, CHUNK), CHUNK)
            image = stay_ref[at, across] + up_in[n, inner, :].astype(f32)
            image = masked(image + low_in[n, inner, :].astype(f32), start, h * COLS)
            image_ref[at, across] = image
            return at, across, image

        own = [zero] * MATVECS
        share = width // (pieces // tiles) // CHUNK
        for t in range(tiles):
            rows = pl.ds(t * ROWS, ROWS)
            if halves > 1:
                @pl.when(k > 0)
                def _():
                    for h in range(halves - 1):
                        left_part(k, t, h)
            left_part(k, t, halves - 1)
            for h in range(halves):
                n = k * pieces + t * halves + h
                across = pl.ds(h * COLS, COLS)
                for i in range(channels):
                    w = order_ref[i]
                    term = lax.dot_general(
                        lx_ref[w, rows, :], right_ref[w, across, :], (((1,), (1,)), ((), ())),
                        preferred_element_type=f32,
                    )
                    prefix_ref[i + 1] = prefix_ref[i] + term
                    if t == 0 and i < share:
                        at = pl.ds((h * share + i) * CHUNK, CHUNK)
                        lifted = basis_ref[k, at, :].astype(f32) * pinv_ref[at, :]
                        own = [
                            own[j] + fold(basis_ref[j, at, :].astype(f32) * lifted)
                            for j in range(MATVECS)
                        ]
                first = prefix_ref[raising]
                second = prefix_ref[moving]
                up_out[n] = first.astype(bf16)
                low_out[n] = (second - first).astype(bf16)
                pl.when(has_above)(lambda: up_copy(n).start())
                pl.when(has_below)(lambda: low_copy(n).start())
                stay_ref[rows, across] = prefix_ref[channels] - second

        def finish_step(kk):
            some = range(kk + 1)

            @pl.when(has_below)
            def _():
                basis_above(k).wait_recv()

            @pl.when(has_above)
            def _():
                basis_below(k).wait_recv()

            def sent(h):
                n = k * pieces + (tiles - 1) * halves + h
                across = pl.ds(h * COLS, COLS)

                def body(c, carry):
                    inner = pl.ds(pl.multiple_of(c * CHUNK, CHUNK), CHUNK)
                    at = pl.ds(pl.multiple_of(edge + c * CHUNK, CHUNK), CHUNK)
                    stay = stay_ref[at, across]
                    up = up_out[n, inner, :].astype(f32)
                    low = low_out[n, inner, :].astype(f32)
                    stay_lifted = stay * pinv_ref[at, across]
                    up_lifted = up * up_pinv[inner, across]
                    low_lifted = low * low_pinv[inner, across]
                    new = []
                    for j in some:
                        mine = basis_ref[j, at, across].astype(f32)
                        over = up_basis[j, inner, across].astype(f32)
                        under = low_basis[j, inner, across].astype(f32)
                        new.append(fold(mine * stay + over * up + under * low))
                        new.append(
                            fold(mine * stay_lifted + over * up_lifted + under * low_lifted)
                        )
                    return tuple(a + b for a, b in zip(carry, new))

                return body

            carry = (zero,) * (2 * kk + 2)
            for h in range(halves):
                carry = lax.fori_loop(0, ROWS // CHUNK, sent(h), carry)

            def received(piece):
                def body(c, carry):
                    at, across, image = arrived(piece, c)
                    lifted = image * pinv_ref[at, across]
                    new = []
                    for j in some:
                        vector = basis_ref[j, at, across].astype(f32)
                        new.append(fold(vector * image))
                        new.append(fold(vector * lifted))
                    return tuple(a + b for a, b in zip(carry, new))

                return body

            for piece in range(pieces - halves):
                gather(piece)
                carry = lax.fori_loop(0, ROWS // CHUNK, received(piece), carry)

            parts = {3 * MATVECS: norm_ref[...]}
            for j in some:
                parts[j] = carry[2 * j]
                parts[MATVECS + j] = carry[2 * j + 1]
                parts[2 * MATVECS + j] = own[j]
            publish(kk, parts)

            for piece in range(pieces - halves, pieces):
                gather(piece)

                @pl.loop(0, ROWS // CHUNK)
                def _(c):
                    arrived(piece, c)

            entry = collect(kk)
            scale = lax.rsqrt(entry(3 * MATVECS) + EPS)
            scale_ref[kk] = scale
            scales = [scale_ref[j] for j in range(kk)] + [scale]
            raw = [entry(j) for j in some]
            theta = scale * scale * raw[kk]
            drop = scale * theta
            coefficients = [
                scales[j] * scales[j] * scale
                * (entry(MATVECS + j) - theta * entry(2 * MATVECS + j))
                for j in some
            ]

            def update(c, carry):
                at = pl.ds(pl.multiple_of(c * CHUNK, CHUNK), CHUNK)
                for h in range(halves):
                    across = pl.ds(h * COLS, COLS)

                    def wide(tile):
                        return spread(tile, CHUNK, COLS)

                    image = image_ref[at, across] * wide(scale)
                    if kk == MATVECS - 1:
                        image_ref[at, across] = image
                    vectors = [basis_ref[j, at, across].astype(f32) for j in some]
                    remain = (image - wide(drop) * vectors[kk]) * pinv_ref[at, across]
                    for j in some:
                        remain = remain - wide(coefficients[j]) * vectors[j]
                    if kk == MATVECS - 1:
                        remain_ref[at, across] = remain
                    else:
                        basis_ref[kk + 1, at, across] = remain.astype(bf16)
                    carry = carry + fold(remain * remain)
                return carry

            square = lax.fori_loop(edge // CHUNK, width // CHUNK, update, zero)
            if kk < MATVECS - 1:
                pl.when(has_above)(lambda: basis_above(kk + 1).start())
                pl.when(has_below)(lambda: basis_below(kk + 1).start())
            norm_ref[...] = lax.fori_loop(0, edge // CHUNK, update, square)
            proj = proj_ref[...]
            for j in some:
                proj = jnp.where((line == j) & (lane == kk), scales[j] * scale * raw[j], proj)
            proj_ref[...] = proj

        for kk in range(MATVECS):
            pl.when(k == kk)(functools.partial(finish_step, kk))

    publish(MATVECS, {0: norm_ref[...]})
    store_image = pltpu.make_async_copy(image_ref, image_hbm, store_sem.at[0])
    store_image.start()
    projected_ref[...] = proj_ref[:MATVECS, :MATVECS]

    send_inv.wait_send()
    for h in range(halves):
        send_block(h).wait_send()

    @pl.when(has_above)
    def _():
        to_above.wait_send()

        @pl.loop(0, MATVECS * pieces)
        def _(n):
            up_copy(n).wait_send()

        @pl.loop(0, MATVECS)
        def _(k):
            basis_above(k).wait_send()

    @pl.when(has_below)
    def _():
        to_below.wait_send()

        @pl.loop(0, MATVECS * pieces)
        def _(n):
            low_copy(n).wait_send()

        @pl.loop(0, MATVECS)
        def _(k):
            basis_below(k).wait_send()

    entry = collect(MATVECS)
    scale = lax.rsqrt(entry(0) + EPS)

    def store(t):
        rows = pl.ds(t * ROWS, ROWS)
        return pltpu.make_async_copy(
            following_ref.at[rows, :], next_hbm.at[rows, :], store_sem.at[1 + t]
        )

    for t in range(tiles):
        @pl.loop(t * ROWS // CHUNK, (t + 1) * ROWS // CHUNK)
        def _(c):
            at = pl.ds(pl.multiple_of(c * CHUNK, CHUNK), CHUNK)
            following_ref[at, :] = (
                remain_ref[at, :] * spread(scale, CHUNK, width)
            ).astype(bf16)

        store(t).start()

    @pl.loop(0, MATVECS + 1)
    def _(r):
        sent = slots_ref.at[r, pl.ds(0, secs - 1)]
        pltpu.make_async_copy(sent, sent, sum_send.at[r]).wait()

    store_image.wait()
    for t in range(tiles):
        store(t).wait()


def finish(next_in, image_in, projected_in, next_ref, image_ref, projected_ref, sems):
    pairs = [(next_in, next_ref), (image_in, image_ref), (projected_in, projected_ref)]
    copies = [
        pltpu.make_async_copy(src, dst, sems.at[i]) for i, (src, dst) in enumerate(pairs)
    ]
    for copy in copies:
        copy.start()
    for copy in copies:
        copy.wait()


def per_device(
    left_env, right_env, left_block, right_block, inv_sv, precond, sector_dims, channel_charge
):
    segs, secs = lax.axis_size("seg"), lax.axis_size("sec")
    channels, width = left_env.shape[2], left_env.shape[-1]
    tiles, halves = width // ROWS, width // COLS
    halos = MATVECS * tiles * halves
    f32, bf16 = jnp.float32, jnp.bfloat16
    vmem = pl.BlockSpec(memory_space=pltpu.VMEM)
    smem = pl.BlockSpec(memory_space=pltpu.SMEM)
    hbm = pl.BlockSpec(memory_space=pl.ANY)
    out_shape = (
        jax.ShapeDtypeStruct((width, width), bf16),
        jax.ShapeDtypeStruct((width, width), f32),
        jax.ShapeDtypeStruct((MATVECS, MATVECS), f32),
    )
    dma = pltpu.SemaphoreType.DMA
    results = pl.pallas_call(
        functools.partial(kernel, segs, secs),
        name="davidson",
        out_shape=out_shape,
        in_specs=[smem, smem, hbm, hbm, hbm, hbm, vmem, hbm],
        out_specs=(hbm, hbm, vmem),
        scratch_shapes=[
            pltpu.VMEM((channels, width, width), bf16),
            pltpu.VMEM((channels, width, width), bf16),
            pltpu.VMEM((width, width), bf16),
            pltpu.VMEM((width, width), f32),
            pltpu.VMEM((width, width), bf16),
            pltpu.VMEM((1, width), bf16),
            pltpu.VMEM((width, width), bf16),
            pltpu.VMEM((MATVECS, width, width), bf16),
            pltpu.VMEM((MATVECS, ROWS, width), bf16),
            pltpu.VMEM((MATVECS, ROWS, width), bf16),
            pltpu.VMEM((ROWS, width), f32),
            pltpu.VMEM((ROWS, width), f32),
            pltpu.VMEM((channels, width, width), bf16),
            pltpu.VMEM((channels + 1, ROWS, COLS), f32),
            pltpu.VMEM((width, width), f32),
            pltpu.VMEM((halos, ROWS, COLS), bf16),
            pltpu.VMEM((halos, ROWS, COLS), bf16),
            pltpu.VMEM((halos, ROWS, COLS), bf16),
            pltpu.VMEM((halos, ROWS, COLS), bf16),
            pltpu.VMEM((width, width), f32),
            pltpu.VMEM((width, width), f32),
            pltpu.VMEM((width, width), bf16),
            pltpu.VMEM((MATVECS + 1, secs, 1, 128), f32),
            pltpu.VMEM((8, 128), f32),
            pltpu.VMEM((MATVECS, 8, 128), f32),
            pltpu.VMEM((8, 128), f32),
            pltpu.SMEM((channels,), jnp.int32),
            dma((4,)),
            dma((1 + halves,)),
            dma((1 + halves,)),
            dma((2,)),
            dma((2,)),
            dma((2, halos)),
            dma((2, halos)),
            dma((2, MATVECS)),
            dma((2, MATVECS)),
            dma((MATVECS + 1,)),
            dma((MATVECS + 1,)),
            dma((1 + tiles,)),
        ],
        compiler_params=pltpu.CompilerParams(
            collective_id=0, has_side_effects=True, vmem_limit_bytes=60 * 1024 * 1024
        ),
    )(
        channel_charge, sector_dims[0, 0], left_env[0, 0], right_env[0, 0],
        left_block[0, 0], right_block[0, 0], inv_sv[0], precond[0, 0],
    )
    following, image, projected = pl.pallas_call(
        finish, name="finish", out_shape=out_shape,
        in_specs=[hbm] * 3, out_specs=(hbm, hbm, hbm),
        scratch_shapes=[dma((3,))],
    )(*results)
    return following[None, None], image[None, None], projected[None]


def solution(mesh):
    in_specs = (
        P("seg", "sec", None, None, None),
        P("seg", "sec", None, None, None),
        P("seg", "sec", None, None),
        P("seg", "sec", None, None),
        P("seg", "sec", None),
        P("seg", "sec", None, None),
        P("seg", "sec", None),
        P(),
    )
    out_specs = (P("seg", "sec", None, None), P("seg", "sec", None, None), P("seg", None, None))
    return jax.shard_map(
        per_device, mesh=mesh, in_specs=in_specs, out_specs=out_specs, check_vma=False
    )
```

```python
import functools

import jax
import jax.numpy as jnp
from jax import lax
from jax.experimental import pallas as pl
from jax.experimental.pallas import tpu as pltpu
from jax.sharding import PartitionSpec as P

MATVECS = 4
EPS = 1e-06
ROWS = 256
COLS = 256
CHUNK = 32
NORM = 3 * MATVECS
MESH = pl.DeviceIdType.MESH


def fold(values):
    rows, columns = values.shape
    block = jnp.sum(values.reshape(rows // 8, 8, columns), axis=0)
    total = block[:, :128]
    for at in range(128, columns, 128):
        total = total + block[:, at : at + 128]
    return total


def spread(tile, rows, columns):
    wide = jnp.concatenate([tile] * (columns // 128), axis=1)
    return jnp.concatenate([wide] * (rows // 8), axis=0)


def kernel(
    segs, secs,
    charge_ref, dims_ref, left_hbm, right_hbm, block_hbm, other_hbm, inv_ref, precond_hbm,
    next_hbm, image_hbm, projected_ref,
    left_ref, right_ref, block_ref, pinv_ref, nb_ref, ninv_ref, scaled_ref, basis_ref,
    up_basis, low_basis, up_pinv, low_pinv, lx_ref, prefix_ref,
    stay_ref, up_out, low_out, up_in, low_in, image_ref, remain_ref, following_ref,
    slots_ref, norm_ref, own_ref, early_ref, cross_ref, scale_ref, proj_ref, order_ref,
    load_sem, guess_send, guess_recv, pinv_send, pinv_recv, halo_send, halo_recv,
    first_send, first_recv, edge_send, edge_recv, sum_send, sum_recv, store_sem,
):
    channels, width, _ = left_ref.shape
    tiles = width // ROWS
    halves = width // COLS
    pieces = tiles * halves
    edge = width - ROWS
    count = secs * width * width
    f32, bf16 = jnp.float32, jnp.bfloat16
    seg, sec = lax.axis_index("seg"), lax.axis_index("sec")
    seg_before = lax.rem(seg + segs - 1, segs)
    seg_after = lax.rem(seg + 1, segs)
    above = (seg, lax.rem(sec + 1, secs))
    below = (seg, lax.rem(sec + secs - 1, secs))
    has_above = sec < secs - 1
    has_below = sec > 0
    edge_rows = pl.ds(edge, ROWS)

    load_left = pltpu.make_async_copy(left_hbm, left_ref, load_sem.at[0])
    load_right = pltpu.make_async_copy(right_hbm, right_ref, load_sem.at[1])
    load_block = pltpu.make_async_copy(block_hbm, block_ref, load_sem.at[2])
    load_precond = pltpu.make_async_copy(precond_hbm, pinv_ref, load_sem.at[3])
    load_precond.start()
    load_block.start()
    load_left.start()
    load_right.start()

    barrier = pltpu.get_barrier_semaphore()
    pl.semaphore_signal(barrier, inc=1, device_id=(seg_before, sec), device_id_type=MESH)
    pl.semaphore_signal(barrier, inc=1, device_id=(seg_after, sec), device_id_type=MESH)
    for offset in range(1, secs):
        peer = lax.rem(sec + offset, secs)
        pl.semaphore_signal(barrier, inc=1, device_id=(seg, peer), device_id_type=MESH)
    pl.semaphore_wait(barrier, secs + 1)

    def remote(src, dst, send, recv, device):
        return pltpu.make_async_remote_copy(
            src_ref=src, dst_ref=dst, send_sem=send, recv_sem=recv,
            device_id=device, device_id_type=MESH,
        )

    send_inv = remote(
        inv_ref, ninv_ref, guess_send.at[0], guess_recv.at[0], (seg_before, sec)
    )

    def send_block(h):
        across = pl.ds(h * COLS, COLS)
        return remote(
            other_hbm.at[:, across], nb_ref.at[:, across],
            guess_send.at[h + 1], guess_recv.at[h + 1], (seg_before, sec),
        )

    send_inv.start()
    for h in range(halves):
        send_block(h).start()

    to_above = remote(
        precond_hbm.at[edge_rows, :], low_pinv, pinv_send.at[0], pinv_recv.at[0], above
    )
    to_below = remote(
        precond_hbm.at[edge_rows, :], up_pinv, pinv_send.at[1], pinv_recv.at[1], below
    )

    def first_above(h):
        across = pl.ds(h * COLS, COLS)
        return remote(
            basis_ref.at[0, edge_rows, across], low_basis.at[0, :, across],
            first_send.at[0, h], first_recv.at[0, h], above,
        )

    def first_below(h):
        across = pl.ds(h * COLS, COLS)
        return remote(
            basis_ref.at[0, edge_rows, across], up_basis.at[0, :, across],
            first_send.at[1, h], first_recv.at[1, h], below,
        )

    def basis_above(k):
        return remote(
            basis_ref.at[k, edge_rows, :], low_basis.at[k],
            edge_send.at[0, k], edge_recv.at[0, k], above,
        )

    def basis_below(k):
        return remote(
            basis_ref.at[k, edge_rows, :], up_basis.at[k],
            edge_send.at[1, k], edge_recv.at[1, k], below,
        )

    def up_copy(n):
        return remote(
            up_out.at[n], up_in.at[n], halo_send.at[0, n], halo_recv.at[0, n], above
        )

    def low_copy(n):
        return remote(
            low_out.at[n], low_in.at[n], halo_send.at[1, n], halo_recv.at[1, n], below
        )

    pl.when(has_above)(lambda: to_above.start())
    pl.when(has_below)(lambda: to_below.start())

    keys = []
    for w in range(channels):
        q = charge_ref[w]
        keys.append(jnp.where(q == 1, 0, jnp.where(q == -1, 1, 2)))
    raising = jnp.int32(0)
    moving = jnp.int32(0)
    for w in range(channels):
        raising = raising + jnp.where(keys[w] == 0, 1, 0)
        moving = moving + jnp.where(keys[w] <= 1, 1, 0)
    places = []
    for w in range(channels):
        place = jnp.int32(0)
        for v in range(channels):
            if v < w:
                place = place + jnp.where(keys[v] <= keys[w], 1, 0)
            elif v > w:
                place = place + jnp.where(keys[v] < keys[w], 1, 0)
        places.append(place)
    for i in range(channels):
        who = jnp.int32(0)
        for w in range(channels):
            who = who + jnp.where(places[w] == i, w, 0)
        order_ref[i] = who

    proj_ref[...] = jnp.zeros_like(proj_ref)

    def chunked(rows, body):
        @pl.loop(0, rows // CHUNK)
        def _(c):
            body(pl.ds(pl.multiple_of(c * CHUNK, CHUNK), CHUNK))

    def clear(at):
        for k in range(1, MATVECS):
            basis_ref[k, at, :] = jnp.zeros((CHUNK, width), bf16)

    def clear_prefix(at):
        prefix_ref[0, at, :] = jnp.zeros((CHUNK, COLS), f32)

    def clear_edges(at):
        for k in range(1, MATVECS):
            up_basis[k, at, :] = jnp.zeros((CHUNK, width), bf16)
            low_basis[k, at, :] = jnp.zeros((CHUNK, width), bf16)

    chunked(width, clear)
    chunked(ROWS, clear_edges)
    chunked(ROWS, clear_prefix)

    def no_neighbour(halo, vectors, inverse):
        @pl.loop(0, MATVECS * pieces)
        def _(n):
            halo[n] = jnp.zeros((ROWS, COLS), bf16)

        vectors[0] = jnp.zeros((ROWS, width), bf16)
        inverse[...] = jnp.ones((ROWS, width), f32)

    pl.when(sec == 0)(lambda: no_neighbour(up_in, low_basis, low_pinv))
    pl.when(sec == secs - 1)(lambda: no_neighbour(low_in, up_basis, up_pinv))

    def invert(ref):
        def body(at):
            ref[at, :] = 1.0 / ref[at, :]

        chunked(ref.shape[0], body)

    load_precond.wait()
    invert(pinv_ref)

    def masked(values, start, left=0):
        row = start + lax.broadcasted_iota(jnp.int32, values.shape, 0)
        column = left + lax.broadcasted_iota(jnp.int32, values.shape, 1)
        inside = (row < dims_ref[0]) & (column < dims_ref[1])
        return jnp.where(inside, values, 0.0)

    lane = lax.broadcasted_iota(jnp.int32, (8, 128), 1)
    line = lax.broadcasted_iota(jnp.int32, (8, 128), 0)
    zero = jnp.zeros((8, 128), f32)

    def sum_copies(r):
        own = slots_ref.at[r, sec]
        return [
            remote(
                own, own, sum_send.at[r], sum_recv.at[r],
                (seg, lax.rem(sec + offset, secs)),
            )
            for offset in range(1, secs)
        ]

    def publish(r, parts):
        tile = zero
        for at, part in parts.items():
            tile = jnp.where(lane == at, jnp.sum(part, axis=1, keepdims=True), tile)
        slots_ref[r, sec] = jnp.sum(tile, axis=0, keepdims=True)
        for copy in sum_copies(r):
            copy.start()

    def collect(r):
        arrived = slots_ref.at[r, pl.ds(0, secs - 1)]
        pltpu.make_async_copy(arrived, arrived, sum_recv.at[r]).wait()
        total = jnp.sum(slots_ref[r], axis=0) * (1.0 / count)
        total = jnp.broadcast_to(total, (8, 128))

        def entry(at):
            value = jnp.sum(jnp.where(lane == at, total, 0.0), axis=1, keepdims=True)
            return jnp.broadcast_to(value, (8, 128))

        return entry

    def left_part(k, t, h):
        rows, across = pl.ds(t * ROWS, ROWS), pl.ds(h * COLS, COLS)
        vector = basis_ref[k, :, across]
        for w in range(channels):
            lx_ref[w, rows, across] = jnp.dot(
                left_ref[w, rows, :], vector, preferred_element_type=f32
            ).astype(bf16)

    send_inv.wait_recv()
    load_block.wait()
    scaled_ref[...] = (
        block_ref[...].astype(f32) * ninv_ref[...].astype(f32)
    ).astype(bf16)

    for h in range(halves):
        across = pl.ds(h * COLS, COLS)
        send_block(h).wait_recv()
        for t in range(tiles):
            rows = pl.ds(t * ROWS, ROWS)
            guess = masked(
                jnp.dot(
                    scaled_ref[rows, :], nb_ref[:, across], preferred_element_type=f32
                ),
                t * ROWS, h * COLS,
            )
            basis_ref[0, rows, across] = guess.astype(bf16)
        pl.when(has_above)(lambda: first_above(h).start())
        pl.when(has_below)(lambda: first_below(h).start())
        if h == 0:
            load_left.wait()
        if h < halves - 1:
            for t in range(tiles):
                left_part(0, t, h)
        if h == 0:
            @pl.when(has_below)
            def _():
                to_above.wait_recv()

            @pl.when(has_above)
            def _():
                to_below.wait_recv()

            invert(up_pinv)
            invert(low_pinv)
            load_right.wait()

    def edge_sums(k, h, c, some):
        n = k * pieces + (tiles - 1) * halves + h
        across = pl.ds(h * COLS, COLS)
        if isinstance(c, int):
            inner, at = pl.ds(c * CHUNK, CHUNK), pl.ds(edge + c * CHUNK, CHUNK)
        else:
            inner = pl.ds(pl.multiple_of(c * CHUNK, CHUNK), CHUNK)
            at = pl.ds(pl.multiple_of(edge + c * CHUNK, CHUNK), CHUNK)
        stay = stay_ref[at, across]
        up = up_out[n, inner, :].astype(f32)
        low = low_out[n, inner, :].astype(f32)

        def three(j):
            return (
                basis_ref[j, at, across].astype(f32),
                up_basis[j, inner, across].astype(f32),
                low_basis[j, inner, across].astype(f32),
            )

        mine, over, under = three(k)
        sums = [fold(mine * stay + over * up + under * low)]
        stay = stay * pinv_ref[at, across]
        up = up * up_pinv[inner, across]
        low = low * low_pinv[inner, across]
        for j in some:
            mine, over, under = three(j)
            sums.append(fold(mine * stay + over * up + under * low))
        return sums

    def edge_arrived(k):
        @pl.when(has_below)
        def _():
            basis_above(k).wait_recv()

        @pl.when(has_above)
        def _():
            basis_below(k).wait_recv()

    def first_arrived():
        for h in range(halves):
            @pl.when(has_below)
            def _():
                first_above(h).wait_recv()

            @pl.when(has_above)
            def _():
                first_below(h).wait_recv()

    def portion(i, total):
        return range(i * total // channels, (i + 1) * total // channels)

    def product(k, first=False):
        own = [zero] * (MATVECS + 1)
        early = [zero] * (MATVECS + 1)
        for t in range(tiles):
            rows = pl.ds(t * ROWS, ROWS)
            for h in range(halves - 1 if first else 0, halves):
                left_part(k, t, h)
            for h in range(halves):
                n = k * pieces + t * halves + h
                across = pl.ds(h * COLS, COLS)
                for i in range(channels):
                    w = order_ref[i]
                    term = lax.dot_general(
                        lx_ref[w, rows, :], right_ref[w, across, :], (((1,), (1,)), ((), ())),
                        preferred_element_type=f32,
                    )
                    prefix_ref[i + 1] = prefix_ref[i] + term
                    if t == 0:
                        share = width // CHUNK // halves
                        for c in portion(i, share):
                            at = pl.ds((h * share + c) * CHUNK, CHUNK)
                            current = basis_ref[k, at, :].astype(f32)
                            lifted = current * pinv_ref[at, :]
                            for j in range(MATVECS):
                                vector = basis_ref[j, at, :].astype(f32)
                                own[j] = own[j] + fold(vector * lifted)
                            own[MATVECS] = own[MATVECS] + fold(current * current)
                    if t == tiles - 1 and h > 0:
                        for c in portion(i, ROWS // CHUNK):
                            sums = edge_sums(k, h - 1, c, range(MATVECS))
                            early = [a + b for a, b in zip(early, sums)]
                first_sum = prefix_ref[raising]
                second_sum = prefix_ref[moving]
                up_out[n] = first_sum.astype(bf16)
                low_out[n] = (second_sum - first_sum).astype(bf16)
                pl.when(has_above)(lambda: up_copy(n).start())
                pl.when(has_below)(lambda: low_copy(n).start())
                stay_ref[rows, across] = prefix_ref[channels] - second_sum
                if t == tiles - 1 and h == 0:
                    if first:
                        first_arrived()
                    else:
                        edge_arrived(k)
        for j in range(MATVECS + 1):
            own_ref[j] = own[j]
            early_ref[j] = early[j]

    product(0, True)

    @pl.loop(0, MATVECS)
    def _(k):
        def gather(piece):
            n = k * pieces + piece

            @pl.when(has_below)
            def _():
                up_copy(n).wait_recv()

            @pl.when(has_above)
            def _():
                low_copy(n).wait_recv()

        def arrived(piece, c):
            t, h = divmod(piece, halves)
            n = k * pieces + piece
            across = pl.ds(h * COLS, COLS)
            inner = pl.ds(pl.multiple_of(c * CHUNK, CHUNK), CHUNK)
            start = t * ROWS + c * CHUNK
            at = pl.ds(pl.multiple_of(start, CHUNK), CHUNK)
            image = stay_ref[at, across] + up_in[n, inner, :].astype(f32)
            image = masked(image + low_in[n, inner, :].astype(f32), start, h * COLS)
            image_ref[at, across] = image
            return at, across, image

        def finish_step(kk):
            some = range(kk + 1)
            past = range(kk)

            def add(carry, new):
                return tuple(a + b for a, b in zip(carry, new))

            def sent(c, carry):
                return add(carry, edge_sums(kk, halves - 1, c, some))

            carry = tuple(early_ref[j] for j in range(kk + 2))
            carry = lax.fori_loop(0, ROWS // CHUNK, sent, carry)

            def received(piece):
                def body(c, carry):
                    at, across, image = arrived(piece, c)
                    lifted = image * pinv_ref[at, across]
                    vectors = [basis_ref[j, at, across].astype(f32) for j in some]
                    new = [fold(vectors[kk] * image)]
                    new += [fold(vector * lifted) for vector in vectors]
                    return add(carry, new)

                return body

            for piece in range(pieces - halves):
                gather(piece)
                carry = lax.fori_loop(0, ROWS // CHUNK, received(piece), carry)

            parts = {0: carry[0], NORM: own_ref[MATVECS]}
            for j in some:
                parts[MATVECS + j] = carry[1 + j]
                parts[2 * MATVECS + j] = own_ref[j]
            for j in range(kk - 1):
                parts[NORM + 1 + j] = cross_ref[j]
            publish(kk, parts)

            def crossed(c, carry):
                at = pl.ds(pl.multiple_of(c * CHUNK, CHUNK), CHUNK)
                return add(
                    carry,
                    [fold(basis_ref[j, at, :].astype(f32) * image_ref[at, :]) for j in past],
                )

            cross = (zero,) * kk
            if kk:
                cross = lax.fori_loop(0, edge // CHUNK, crossed, cross)

            for piece in range(pieces - halves, pieces):
                gather(piece)

                def land(c, carry):
                    at, across, image = arrived(piece, c)
                    return add(
                        carry,
                        [fold(basis_ref[j, at, across].astype(f32) * image) for j in past],
                    )

                cross = lax.fori_loop(0, ROWS // CHUNK, land, cross)

            entry = collect(kk)
            scale = lax.rsqrt(entry(NORM) + EPS)
            scales = [scale_ref[j] for j in past] + [scale]
            diagonal = scale * scale * entry(0)
            drop = scale * diagonal
            coefficients = [
                scales[j] * scales[j] * scale
                * (entry(MATVECS + j) - diagonal * entry(2 * MATVECS + j))
                for j in some
            ]

            def update(c, carry):
                at = pl.ds(pl.multiple_of(c * CHUNK, CHUNK), CHUNK)
                for h in range(halves):
                    across = pl.ds(h * COLS, COLS)

                    def wide(tile):
                        return spread(tile, CHUNK, COLS)

                    image = image_ref[at, across] * wide(scale)
                    if kk == MATVECS - 1:
                        image_ref[at, across] = image
                    vectors = [basis_ref[j, at, across].astype(f32) for j in some]
                    remain = (image - wide(drop) * vectors[kk]) * pinv_ref[at, across]
                    for j in some:
                        remain = remain - wide(coefficients[j]) * vectors[j]
                    if kk == MATVECS - 1:
                        remain_ref[at, across] = remain
                        carry = carry + fold(remain * remain)
                    else:
                        basis_ref[kk + 1, at, across] = remain.astype(bf16)
                return carry

            square = lax.fori_loop(edge // CHUNK, width // CHUNK, update, zero)
            if kk < MATVECS - 1:
                pl.when(has_above)(lambda: basis_above(kk + 1).start())
                pl.when(has_below)(lambda: basis_below(kk + 1).start())
            square = lax.fori_loop(0, edge // CHUNK, update, square)
            if kk == MATVECS - 1:
                norm_ref[...] = square
            scale_ref[kk] = scale
            for j in past:
                cross_ref[j] = cross[j]
            proj = jnp.where((line == kk) & (lane == kk), diagonal, proj_ref[...])
            for j in range(kk - 1):
                value = scales[j] * scales[kk - 1] * entry(NORM + 1 + j)
                proj = jnp.where((line == j) & (lane == kk - 1), value, proj)
            proj_ref[...] = proj

        for kk in range(MATVECS):
            pl.when(k == kk)(functools.partial(finish_step, kk))
        pl.when(k < MATVECS - 1)(lambda: product(k + 1))

    last = MATVECS - 1
    parts = {NORM: norm_ref[...]}
    for j in range(last):
        parts[NORM + 1 + j] = cross_ref[j]
    publish(MATVECS, parts)
    store_image = pltpu.make_async_copy(image_ref, image_hbm, store_sem.at[0])
    store_image.start()

    send_inv.wait_send()
    for h in range(halves):
        send_block(h).wait_send()

    @pl.when(has_above)
    def _():
        to_above.wait_send()

        @pl.loop(0, MATVECS * pieces)
        def _(n):
            up_copy(n).wait_send()

        for h in range(halves):
            first_above(h).wait_send()

        @pl.loop(1, MATVECS)
        def _(k):
            basis_above(k).wait_send()

    @pl.when(has_below)
    def _():
        to_below.wait_send()

        @pl.loop(0, MATVECS * pieces)
        def _(n):
            low_copy(n).wait_send()

        for h in range(halves):
            first_below(h).wait_send()

        @pl.loop(1, MATVECS)
        def _(k):
            basis_below(k).wait_send()

    entry = collect(MATVECS)
    scale = lax.rsqrt(entry(NORM) + EPS)

    def store(t):
        rows = pl.ds(t * ROWS, ROWS)
        return pltpu.make_async_copy(
            following_ref.at[rows, :], next_hbm.at[rows, :], store_sem.at[1 + t]
        )

    for t in range(tiles):
        @pl.loop(t * ROWS // CHUNK, (t + 1) * ROWS // CHUNK)
        def _(c):
            at = pl.ds(pl.multiple_of(c * CHUNK, CHUNK), CHUNK)
            following_ref[at, :] = (
                remain_ref[at, :] * spread(scale, CHUNK, width)
            ).astype(bf16)

        store(t).start()

    proj = proj_ref[...]
    for j in range(last):
        value = scale_ref[j] * scale_ref[last] * entry(NORM + 1 + j)
        proj = jnp.where((line == j) & (lane == last), value, proj)
    projected_ref[...] = proj[:MATVECS, :MATVECS]

    @pl.loop(0, MATVECS + 1)
    def _(r):
        sent = slots_ref.at[r, pl.ds(0, secs - 1)]
        pltpu.make_async_copy(sent, sent, sum_send.at[r]).wait()

    store_image.wait()
    for t in range(tiles):
        store(t).wait()


def finish(next_in, image_in, projected_in, next_ref, image_ref, projected_ref):
    next_ref[...] = next_in[...]
    image_ref[...] = image_in[...]
    projected_ref[...] = projected_in[...]


def per_device(
    left_env, right_env, left_block, right_block, inv_sv, precond, sector_dims, channel_charge
):
    segs, secs = lax.axis_size("seg"), lax.axis_size("sec")
    channels, width = left_env.shape[2], left_env.shape[-1]
    tiles, halves = width // ROWS, width // COLS
    halos = MATVECS * tiles * halves
    f32, bf16 = jnp.float32, jnp.bfloat16
    vmem = pl.BlockSpec(memory_space=pltpu.VMEM)
    smem = pl.BlockSpec(memory_space=pltpu.SMEM)
    hbm = pl.BlockSpec(memory_space=pl.ANY)
    out_shape = (
        jax.ShapeDtypeStruct((width, width), bf16),
        jax.ShapeDtypeStruct((width, width), f32),
        jax.ShapeDtypeStruct((MATVECS, MATVECS), f32),
    )
    dma = pltpu.SemaphoreType.DMA
    results = pl.pallas_call(
        functools.partial(kernel, segs, secs),
        name="davidson",
        out_shape=out_shape,
        in_specs=[smem, smem, hbm, hbm, hbm, hbm, vmem, hbm],
        out_specs=(hbm, hbm, vmem),
        scratch_shapes=[
            pltpu.VMEM((channels, width, width), bf16),
            pltpu.VMEM((channels, width, width), bf16),
            pltpu.VMEM((width, width), bf16),
            pltpu.VMEM((width, width), f32),
            pltpu.VMEM((width, width), bf16),
            pltpu.VMEM((1, width), bf16),
            pltpu.VMEM((width, width), bf16),
            pltpu.VMEM((MATVECS, width, width), bf16),
            pltpu.VMEM((MATVECS, ROWS, width), bf16),
            pltpu.VMEM((MATVECS, ROWS, width), bf16),
            pltpu.VMEM((ROWS, width), f32),
            pltpu.VMEM((ROWS, width), f32),
            pltpu.VMEM((channels, width, width), bf16),
            pltpu.VMEM((channels + 1, ROWS, COLS), f32),
            pltpu.VMEM((width, width), f32),
            pltpu.VMEM((halos, ROWS, COLS), bf16),
            pltpu.VMEM((halos, ROWS, COLS), bf16),
            pltpu.VMEM((halos, ROWS, COLS), bf16),
            pltpu.VMEM((halos, ROWS, COLS), bf16),
            pltpu.VMEM((width, width), f32),
            pltpu.VMEM((width, width), f32),
            pltpu.VMEM((width, width), bf16),
            pltpu.VMEM((MATVECS + 1, secs, 1, 128), f32),
            pltpu.VMEM((8, 128), f32),
            pltpu.VMEM((MATVECS + 1, 8, 128), f32),
            pltpu.VMEM((MATVECS + 1, 8, 128), f32),
            pltpu.VMEM((MATVECS, 8, 128), f32),
            pltpu.VMEM((MATVECS, 8, 128), f32),
            pltpu.VMEM((8, 128), f32),
            pltpu.SMEM((channels,), jnp.int32),
            dma((4,)),
            dma((1 + halves,)),
            dma((1 + halves,)),
            dma((2,)),
            dma((2,)),
            dma((2, halos)),
            dma((2, halos)),
            dma((2, halves)),
            dma((2, halves)),
            dma((2, MATVECS)),
            dma((2, MATVECS)),
            dma((MATVECS + 1,)),
            dma((MATVECS + 1,)),
            dma((1 + tiles,)),
        ],
        compiler_params=pltpu.CompilerParams(
            collective_id=0, has_side_effects=True, vmem_limit_bytes=60 * 1024 * 1024
        ),
    )(
        channel_charge, sector_dims[0, 0], left_env[0, 0], right_env[0, 0],
        left_block[0, 0], right_block[0, 0], inv_sv[0], precond[0, 0],
    )
    following, image, projected = pl.pallas_call(
        finish, name="finish", out_shape=out_shape,
        in_specs=[vmem] * 3, out_specs=(vmem, vmem, vmem),
    )(*results)
    return following[None, None], image[None, None], projected[None]


def solution(mesh):
    in_specs = (
        P("seg", "sec", None, None, None),
        P("seg", "sec", None, None, None),
        P("seg", "sec", None, None),
        P("seg", "sec", None, None),
        P("seg", "sec", None),
        P("seg", "sec", None, None),
        P("seg", "sec", None),
        P(),
    )
    out_specs = (P("seg", "sec", None, None), P("seg", "sec", None, None), P("seg", None, None))
    return jax.shard_map(
        per_device, mesh=mesh, in_specs=in_specs, out_specs=out_specs, check_vma=False
    )
```

```python
import functools

import jax
import jax.numpy as jnp
from jax import lax
from jax.experimental import pallas as pl
from jax.experimental.pallas import tpu as pltpu
from jax.sharding import PartitionSpec as P

MATVECS = 4
EPS = 1e-06
ROWS = 256
COLS = 256
CHUNK = 32
NORM = 3 * MATVECS
MESH = pl.DeviceIdType.MESH


def fold(values):
    rows, columns = values.shape
    block = jnp.sum(values.reshape(rows // 8, 8, columns), axis=0)
    total = block[:, :128]
    for at in range(128, columns, 128):
        total = total + block[:, at : at + 128]
    return total


def spread(tile, rows, columns):
    wide = jnp.concatenate([tile] * (columns // 128), axis=1)
    return jnp.concatenate([wide] * (rows // 8), axis=0)


def kernel(
    segs, secs,
    charge_ref, dims_ref, left_hbm, right_hbm, block_hbm, other_hbm, inv_ref, precond_hbm,
    next_hbm, image_hbm, projected_ref,
    left_ref, right_ref, block_ref, pinv_ref, nb_ref, ninv_ref, scaled_ref, basis_ref,
    up_basis, low_basis, edge_pinv, up_pinv, low_pinv, lx_ref, prefix_ref,
    stay_ref, up_out, low_out, up_in, low_in, image_ref, remain_ref, following_ref,
    slots_ref, norm_ref, own_ref, early_ref, cross_ref, scale_ref, proj_ref, order_ref,
    load_sem, guess_send, guess_recv, pinv_send, pinv_recv, halo_send, halo_recv,
    first_send, first_recv, edge_send, edge_recv, sum_send, sum_recv, store_sem,
):
    channels, width, _ = left_ref.shape
    tiles = width // ROWS
    halves = width // COLS
    pieces = tiles * halves
    edge = width - ROWS
    count = secs * width * width
    f32, bf16 = jnp.float32, jnp.bfloat16
    seg, sec = lax.axis_index("seg"), lax.axis_index("sec")
    seg_before = lax.rem(seg + segs - 1, segs)
    seg_after = lax.rem(seg + 1, segs)
    above = (seg, lax.rem(sec + 1, secs))
    below = (seg, lax.rem(sec + secs - 1, secs))
    has_above = sec < secs - 1
    has_below = sec > 0
    edge_rows = pl.ds(edge, ROWS)

    load_left = pltpu.make_async_copy(left_hbm, left_ref, load_sem.at[0])
    load_right = pltpu.make_async_copy(right_hbm, right_ref, load_sem.at[1])
    load_block = pltpu.make_async_copy(block_hbm, block_ref, load_sem.at[2])
    load_precond = pltpu.make_async_copy(precond_hbm, pinv_ref, load_sem.at[3])
    load_precond.start()
    load_block.start()
    load_left.start()
    load_right.start()

    barrier = pltpu.get_barrier_semaphore()
    pl.semaphore_signal(barrier, inc=1, device_id=(seg_before, sec), device_id_type=MESH)
    pl.semaphore_signal(barrier, inc=1, device_id=(seg_after, sec), device_id_type=MESH)
    for offset in range(1, secs):
        peer = lax.rem(sec + offset, secs)
        pl.semaphore_signal(barrier, inc=1, device_id=(seg, peer), device_id_type=MESH)
    pl.semaphore_wait(barrier, secs + 1)

    def remote(src, dst, send, recv, device):
        return pltpu.make_async_remote_copy(
            src_ref=src, dst_ref=dst, send_sem=send, recv_sem=recv,
            device_id=device, device_id_type=MESH,
        )

    send_inv = remote(
        inv_ref, ninv_ref, guess_send.at[0], guess_recv.at[0], (seg_before, sec)
    )

    def send_block(h):
        across = pl.ds(h * COLS, COLS)
        return remote(
            other_hbm.at[:, across], nb_ref.at[:, across],
            guess_send.at[h + 1], guess_recv.at[h + 1], (seg_before, sec),
        )

    send_inv.start()
    for h in range(halves):
        send_block(h).start()

    to_above = remote(edge_pinv, low_pinv, pinv_send.at[0], pinv_recv.at[0], above)
    to_below = remote(edge_pinv, up_pinv, pinv_send.at[1], pinv_recv.at[1], below)

    def first_above(h):
        across = pl.ds(h * COLS, COLS)
        return remote(
            basis_ref.at[0, edge_rows, across], low_basis.at[0, :, across],
            first_send.at[0, h], first_recv.at[0, h], above,
        )

    def first_below(h):
        across = pl.ds(h * COLS, COLS)
        return remote(
            basis_ref.at[0, edge_rows, across], up_basis.at[0, :, across],
            first_send.at[1, h], first_recv.at[1, h], below,
        )

    def basis_above(k):
        return remote(
            basis_ref.at[k, edge_rows, :], low_basis.at[k],
            edge_send.at[0, k], edge_recv.at[0, k], above,
        )

    def basis_below(k):
        return remote(
            basis_ref.at[k, edge_rows, :], up_basis.at[k],
            edge_send.at[1, k], edge_recv.at[1, k], below,
        )

    def up_copy(n):
        return remote(
            up_out.at[n], up_in.at[n], halo_send.at[0, n], halo_recv.at[0, n], above
        )

    def low_copy(n):
        return remote(
            low_out.at[n], low_in.at[n], halo_send.at[1, n], halo_recv.at[1, n], below
        )

    keys = []
    for w in range(channels):
        q = charge_ref[w]
        keys.append(jnp.where(q == 1, 0, jnp.where(q == -1, 1, 2)))
    raising = jnp.int32(0)
    moving = jnp.int32(0)
    for w in range(channels):
        raising = raising + jnp.where(keys[w] == 0, 1, 0)
        moving = moving + jnp.where(keys[w] <= 1, 1, 0)
    places = []
    for w in range(channels):
        place = jnp.int32(0)
        for v in range(channels):
            if v < w:
                place = place + jnp.where(keys[v] <= keys[w], 1, 0)
            elif v > w:
                place = place + jnp.where(keys[v] < keys[w], 1, 0)
        places.append(place)
    for i in range(channels):
        who = jnp.int32(0)
        for w in range(channels):
            who = who + jnp.where(places[w] == i, w, 0)
        order_ref[i] = who

    proj_ref[...] = jnp.zeros_like(proj_ref)

    def chunked(rows, body):
        @pl.loop(0, rows // CHUNK)
        def _(c):
            body(pl.ds(pl.multiple_of(c * CHUNK, CHUNK), CHUNK))

    def clear(at):
        for k in range(1, MATVECS):
            basis_ref[k, at, :] = jnp.zeros((CHUNK, width), bf16)

    def clear_prefix(at):
        prefix_ref[0, at, :] = jnp.zeros((CHUNK, COLS), f32)

    def clear_edges(at):
        for k in range(1, MATVECS):
            up_basis[k, at, :] = jnp.zeros((CHUNK, width), bf16)
            low_basis[k, at, :] = jnp.zeros((CHUNK, width), bf16)

    chunked(width, clear)
    chunked(ROWS, clear_edges)
    chunked(ROWS, clear_prefix)

    def no_neighbour(halo, vectors, inverse):
        @pl.loop(0, MATVECS * pieces)
        def _(n):
            halo[n] = jnp.zeros((ROWS, COLS), bf16)

        vectors[0] = jnp.zeros((ROWS, width), bf16)
        inverse[...] = jnp.ones((ROWS, width), bf16)

    pl.when(sec == 0)(lambda: no_neighbour(up_in, low_basis, low_pinv))
    pl.when(sec == secs - 1)(lambda: no_neighbour(low_in, up_basis, up_pinv))

    def masked(values, start, left=0):
        row = start + lax.broadcasted_iota(jnp.int32, values.shape, 0)
        column = left + lax.broadcasted_iota(jnp.int32, values.shape, 1)
        inside = (row < dims_ref[0]) & (column < dims_ref[1])
        return jnp.where(inside, values, 0.0)

    load_precond.wait()

    @pl.loop(0, width // CHUNK)
    def _(c):
        at = pl.ds(pl.multiple_of(c * CHUNK, CHUNK), CHUNK)
        pinv_ref[at, :] = masked(1.0 / pinv_ref[at, :], c * CHUNK)

    @pl.loop(0, ROWS // CHUNK)
    def _(c):
        at = pl.ds(pl.multiple_of(edge + c * CHUNK, CHUNK), CHUNK)
        inner = pl.ds(pl.multiple_of(c * CHUNK, CHUNK), CHUNK)
        edge_pinv[inner, :] = pinv_ref[at, :].astype(bf16)

    pl.when(has_above)(lambda: to_above.start())
    pl.when(has_below)(lambda: to_below.start())

    lane = lax.broadcasted_iota(jnp.int32, (8, 128), 1)
    line = lax.broadcasted_iota(jnp.int32, (8, 128), 0)
    zero = jnp.zeros((8, 128), f32)

    def sum_copies(r):
        own = slots_ref.at[r, sec]
        return [
            remote(
                own, own, sum_send.at[r], sum_recv.at[r],
                (seg, lax.rem(sec + offset, secs)),
            )
            for offset in range(1, secs)
        ]

    def publish(r, parts):
        tile = zero
        for at, part in parts.items():
            tile = jnp.where(lane == at, jnp.sum(part, axis=1, keepdims=True), tile)
        slots_ref[r, sec] = jnp.sum(tile, axis=0, keepdims=True)
        for copy in sum_copies(r):
            copy.start()

    def collect(r):
        arrived = slots_ref.at[r, pl.ds(0, secs - 1)]
        pltpu.make_async_copy(arrived, arrived, sum_recv.at[r]).wait()
        total = jnp.sum(slots_ref[r], axis=0) * (1.0 / count)
        total = jnp.broadcast_to(total, (8, 128))

        def entry(at):
            value = jnp.sum(jnp.where(lane == at, total, 0.0), axis=1, keepdims=True)
            return jnp.broadcast_to(value, (8, 128))

        return entry

    def left_part(k, t, h):
        rows, across = pl.ds(t * ROWS, ROWS), pl.ds(h * COLS, COLS)
        vector = basis_ref[k, :, across]
        for w in range(channels):
            lx_ref[w, rows, across] = jnp.dot(
                left_ref[w, rows, :], vector, preferred_element_type=f32
            ).astype(bf16)

    send_inv.wait_recv()
    load_block.wait()
    scaled_ref[...] = (
        block_ref[...].astype(f32) * ninv_ref[...].astype(f32)
    ).astype(bf16)

    for h in range(halves):
        across = pl.ds(h * COLS, COLS)
        send_block(h).wait_recv()
        for t in range(tiles):
            rows = pl.ds(t * ROWS, ROWS)
            guess = masked(
                jnp.dot(
                    scaled_ref[rows, :], nb_ref[:, across], preferred_element_type=f32
                ),
                t * ROWS, h * COLS,
            )
            basis_ref[0, rows, across] = guess.astype(bf16)
        pl.when(has_above)(lambda: first_above(h).start())
        pl.when(has_below)(lambda: first_below(h).start())
        if h == 0:
            load_left.wait()
        if h < halves - 1:
            for t in range(tiles):
                left_part(0, t, h)
        if h == 0:
            @pl.when(has_below)
            def _():
                to_above.wait_recv()

            @pl.when(has_above)
            def _():
                to_below.wait_recv()

            load_right.wait()

    def edge_sums(k, h, c, some):
        n = k * pieces + (tiles - 1) * halves + h
        across = pl.ds(h * COLS, COLS)
        if isinstance(c, int):
            inner, at = pl.ds(c * CHUNK, CHUNK), pl.ds(edge + c * CHUNK, CHUNK)
        else:
            inner = pl.ds(pl.multiple_of(c * CHUNK, CHUNK), CHUNK)
            at = pl.ds(pl.multiple_of(edge + c * CHUNK, CHUNK), CHUNK)
        stay = stay_ref[at, across]
        up = up_out[n, inner, :].astype(f32)
        low = low_out[n, inner, :].astype(f32)

        def three(j):
            return basis_ref[j, at, across], up_basis[j, inner, across], low_basis[j, inner, across]

        mine, over, under = [vector.astype(f32) for vector in three(k)]
        sums = [fold(mine * stay + over * up + under * low)]
        stay = (stay * pinv_ref[at, across]).astype(bf16)
        up = up_out[n, inner, :] * up_pinv[inner, across]
        low = low_out[n, inner, :] * low_pinv[inner, across]
        for j in some:
            mine, over, under = three(j)
            sums.append(fold((mine * stay + over * up + under * low).astype(f32)))
        return sums

    def edge_arrived(k):
        @pl.when(has_below)
        def _():
            basis_above(k).wait_recv()

        @pl.when(has_above)
        def _():
            basis_below(k).wait_recv()

    def first_arrived():
        for h in range(halves):
            @pl.when(has_below)
            def _():
                first_above(h).wait_recv()

            @pl.when(has_above)
            def _():
                first_below(h).wait_recv()

    def portion(i, total):
        return range(i * total // channels, (i + 1) * total // channels)

    def product(k, first=False):
        own = [zero] * (MATVECS + 1)
        early = [zero] * (MATVECS + 1)
        for t in range(tiles):
            rows = pl.ds(t * ROWS, ROWS)
            for h in range(halves - 1 if first else 0, halves):
                left_part(k, t, h)
            for h in range(halves):
                n = k * pieces + t * halves + h
                across = pl.ds(h * COLS, COLS)
                for i in range(channels):
                    w = order_ref[i]
                    term = lax.dot_general(
                        lx_ref[w, rows, :], right_ref[w, across, :], (((1,), (1,)), ((), ())),
                        preferred_element_type=f32,
                    )
                    prefix_ref[i + 1] = prefix_ref[i] + term
                    if t == 0:
                        share = width // CHUNK // halves
                        for c in portion(i, share):
                            at = pl.ds((h * share + c) * CHUNK, CHUNK)
                            current = basis_ref[k, at, :].astype(f32)
                            lifted = current * pinv_ref[at, :]
                            for j in range(MATVECS):
                                vector = basis_ref[j, at, :].astype(f32)
                                own[j] = own[j] + fold(vector * lifted)
                            own[MATVECS] = own[MATVECS] + fold(current * current)
                    if t == tiles - 1 and h > 0:
                        for c in portion(i, ROWS // CHUNK):
                            sums = edge_sums(k, h - 1, c, range(MATVECS))
                            early = [a + b for a, b in zip(early, sums)]
                first_sum = prefix_ref[raising]
                second_sum = prefix_ref[moving]
                up_out[n] = first_sum.astype(bf16)
                low_out[n] = (second_sum - first_sum).astype(bf16)
                pl.when(has_above)(lambda: up_copy(n).start())
                pl.when(has_below)(lambda: low_copy(n).start())
                stay_ref[rows, across] = prefix_ref[channels] - second_sum
                if t == tiles - 1 and h == 0:
                    if first:
                        first_arrived()
                    else:
                        edge_arrived(k)
        for j in range(MATVECS + 1):
            own_ref[j] = own[j]
            early_ref[j] = early[j]

    product(0, True)

    @pl.loop(0, MATVECS)
    def _(k):
        def gather(piece):
            n = k * pieces + piece

            @pl.when(has_below)
            def _():
                up_copy(n).wait_recv()

            @pl.when(has_above)
            def _():
                low_copy(n).wait_recv()

        def arrived(piece, c):
            t, h = divmod(piece, halves)
            n = k * pieces + piece
            across = pl.ds(h * COLS, COLS)
            inner = pl.ds(pl.multiple_of(c * CHUNK, CHUNK), CHUNK)
            start = t * ROWS + c * CHUNK
            at = pl.ds(pl.multiple_of(start, CHUNK), CHUNK)
            image = stay_ref[at, across] + up_in[n, inner, :].astype(f32)
            image = image + low_in[n, inner, :].astype(f32)
            image_ref[at, across] = image
            return at, across, image

        def finish_step(kk):
            some = range(kk + 1)
            past = range(kk)

            def add(carry, new):
                return tuple(a + b for a, b in zip(carry, new))

            def sent(c, carry):
                return add(carry, edge_sums(kk, halves - 1, c, some))

            carry = tuple(early_ref[j] for j in range(kk + 2))
            carry = lax.fori_loop(0, ROWS // CHUNK, sent, carry)

            def received(piece):
                def body(c, carry):
                    at, across, image = arrived(piece, c)
                    lifted = image * pinv_ref[at, across]
                    vectors = [basis_ref[j, at, across].astype(f32) for j in some]
                    new = [fold(vectors[kk] * image)]
                    new += [fold(vector * lifted) for vector in vectors]
                    return add(carry, new)

                return body

            for piece in range(pieces - halves):
                gather(piece)
                carry = lax.fori_loop(0, ROWS // CHUNK, received(piece), carry)

            parts = {0: carry[0], NORM: own_ref[MATVECS]}
            for j in some:
                parts[MATVECS + j] = carry[1 + j]
                parts[2 * MATVECS + j] = own_ref[j]
            for j in range(kk - 1):
                parts[NORM + 1 + j] = cross_ref[j]
            publish(kk, parts)

            def crossed(c, carry):
                at = pl.ds(pl.multiple_of(c * CHUNK, CHUNK), CHUNK)
                return add(
                    carry,
                    [fold(basis_ref[j, at, :].astype(f32) * image_ref[at, :]) for j in past],
                )

            cross = (zero,) * kk
            if kk:
                cross = lax.fori_loop(0, edge // CHUNK, crossed, cross)

            for piece in range(pieces - halves, pieces):
                gather(piece)

                def land(c, carry):
                    at, across, image = arrived(piece, c)
                    return add(
                        carry,
                        [fold(basis_ref[j, at, across].astype(f32) * image) for j in past],
                    )

                cross = lax.fori_loop(0, ROWS // CHUNK, land, cross)

            entry = collect(kk)
            scale = lax.rsqrt(entry(NORM) + EPS)
            scales = [scale_ref[j] for j in past] + [scale]
            diagonal = scale * scale * entry(0)
            drop = scale * diagonal
            coefficients = [
                scales[j] * scales[j] * scale
                * (entry(MATVECS + j) - diagonal * entry(2 * MATVECS + j))
                for j in some
            ]

            def update(c, carry):
                at = pl.ds(pl.multiple_of(c * CHUNK, CHUNK), CHUNK)
                for h in range(halves):
                    across = pl.ds(h * COLS, COLS)

                    def wide(tile):
                        return spread(tile, CHUNK, COLS)

                    image = image_ref[at, across] * wide(scale)
                    if kk == MATVECS - 1:
                        image_ref[at, across] = masked(image, c * CHUNK, h * COLS)
                    vectors = [basis_ref[j, at, across].astype(f32) for j in some]
                    remain = (image - wide(drop) * vectors[kk]) * pinv_ref[at, across]
                    for j in some:
                        remain = remain - wide(coefficients[j]) * vectors[j]
                    if kk == MATVECS - 1:
                        remain_ref[at, across] = remain
                        carry = carry + fold(remain * remain)
                    else:
                        basis_ref[kk + 1, at, across] = remain.astype(bf16)
                return carry

            square = lax.fori_loop(edge // CHUNK, width // CHUNK, update, zero)
            if kk < MATVECS - 1:
                pl.when(has_above)(lambda: basis_above(kk + 1).start())
                pl.when(has_below)(lambda: basis_below(kk + 1).start())
            square = lax.fori_loop(0, edge // CHUNK, update, square)
            if kk == MATVECS - 1:
                norm_ref[...] = square
            scale_ref[kk] = scale
            for j in past:
                cross_ref[j] = cross[j]
            proj = jnp.where((line == kk) & (lane == kk), diagonal, proj_ref[...])
            for j in range(kk - 1):
                value = scales[j] * scales[kk - 1] * entry(NORM + 1 + j)
                proj = jnp.where((line == j) & (lane == kk - 1), value, proj)
            proj_ref[...] = proj

        for kk in range(MATVECS):
            pl.when(k == kk)(functools.partial(finish_step, kk))
        pl.when(k < MATVECS - 1)(lambda: product(k + 1))

    last = MATVECS - 1
    parts = {NORM: norm_ref[...]}
    for j in range(last):
        parts[NORM + 1 + j] = cross_ref[j]
    publish(MATVECS, parts)
    store_image = pltpu.make_async_copy(image_ref, image_hbm, store_sem.at[0])
    store_image.start()

    send_inv.wait_send()
    for h in range(halves):
        send_block(h).wait_send()

    @pl.when(has_above)
    def _():
        to_above.wait_send()

        @pl.loop(0, MATVECS * pieces)
        def _(n):
            up_copy(n).wait_send()

        for h in range(halves):
            first_above(h).wait_send()

        @pl.loop(1, MATVECS)
        def _(k):
            basis_above(k).wait_send()

    @pl.when(has_below)
    def _():
        to_below.wait_send()

        @pl.loop(0, MATVECS * pieces)
        def _(n):
            low_copy(n).wait_send()

        for h in range(halves):
            first_below(h).wait_send()

        @pl.loop(1, MATVECS)
        def _(k):
            basis_below(k).wait_send()

    entry = collect(MATVECS)
    scale = lax.rsqrt(entry(NORM) + EPS)

    def store(t):
        rows = pl.ds(t * ROWS, ROWS)
        return pltpu.make_async_copy(
            following_ref.at[rows, :], next_hbm.at[rows, :], store_sem.at[1 + t]
        )

    for t in range(tiles):
        @pl.loop(t * ROWS // CHUNK, (t + 1) * ROWS // CHUNK)
        def _(c):
            at = pl.ds(pl.multiple_of(c * CHUNK, CHUNK), CHUNK)
            following_ref[at, :] = (
                remain_ref[at, :] * spread(scale, CHUNK, width)
            ).astype(bf16)

        store(t).start()

    proj = proj_ref[...]
    for j in range(last):
        value = scale_ref[j] * scale_ref[last] * entry(NORM + 1 + j)
        proj = jnp.where((line == j) & (lane == last), value, proj)
    projected_ref[...] = proj[:MATVECS, :MATVECS]

    @pl.loop(0, MATVECS + 1)
    def _(r):
        sent = slots_ref.at[r, pl.ds(0, secs - 1)]
        pltpu.make_async_copy(sent, sent, sum_send.at[r]).wait()

    store_image.wait()
    for t in range(tiles):
        store(t).wait()


def finish(next_in, image_in, projected_in, next_ref, image_ref, projected_ref):
    next_ref[...] = next_in[...]
    image_ref[...] = image_in[...]
    projected_ref[...] = projected_in[...]


def per_device(
    left_env, right_env, left_block, right_block, inv_sv, precond, sector_dims, channel_charge
):
    segs, secs = lax.axis_size("seg"), lax.axis_size("sec")
    channels, width = left_env.shape[2], left_env.shape[-1]
    tiles, halves = width // ROWS, width // COLS
    halos = MATVECS * tiles * halves
    f32, bf16 = jnp.float32, jnp.bfloat16
    vmem = pl.BlockSpec(memory_space=pltpu.VMEM)
    smem = pl.BlockSpec(memory_space=pltpu.SMEM)
    hbm = pl.BlockSpec(memory_space=pl.ANY)
    out_shape = (
        jax.ShapeDtypeStruct((width, width), bf16),
        jax.ShapeDtypeStruct((width, width), f32),
        jax.ShapeDtypeStruct((MATVECS, MATVECS), f32),
    )
    dma = pltpu.SemaphoreType.DMA
    results = pl.pallas_call(
        functools.partial(kernel, segs, secs),
        name="davidson",
        out_shape=out_shape,
        in_specs=[smem, smem, hbm, hbm, hbm, hbm, vmem, hbm],
        out_specs=(hbm, hbm, vmem),
        scratch_shapes=[
            pltpu.VMEM((channels, width, width), bf16),
            pltpu.VMEM((channels, width, width), bf16),
            pltpu.VMEM((width, width), bf16),
            pltpu.VMEM((width, width), f32),
            pltpu.VMEM((width, width), bf16),
            pltpu.VMEM((1, width), bf16),
            pltpu.VMEM((width, width), bf16),
            pltpu.VMEM((MATVECS, width, width), bf16),
            pltpu.VMEM((MATVECS, ROWS, width), bf16),
            pltpu.VMEM((MATVECS, ROWS, width), bf16),
            pltpu.VMEM((ROWS, width), bf16),
            pltpu.VMEM((ROWS, width), bf16),
            pltpu.VMEM((ROWS, width), bf16),
            pltpu.VMEM((channels, width, width), bf16),
            pltpu.VMEM((channels + 1, ROWS, COLS), f32),
            pltpu.VMEM((width, width), f32),
            pltpu.VMEM((halos, ROWS, COLS), bf16),
            pltpu.VMEM((halos, ROWS, COLS), bf16),
            pltpu.VMEM((halos, ROWS, COLS), bf16),
            pltpu.VMEM((halos, ROWS, COLS), bf16),
            pltpu.VMEM((width, width), f32),
            pltpu.VMEM((width, width), f32),
            pltpu.VMEM((width, width), bf16),
            pltpu.VMEM((MATVECS + 1, secs, 1, 128), f32),
            pltpu.VMEM((8, 128), f32),
            pltpu.VMEM((MATVECS + 1, 8, 128), f32),
            pltpu.VMEM((MATVECS + 1, 8, 128), f32),
            pltpu.VMEM((MATVECS, 8, 128), f32),
            pltpu.VMEM((MATVECS, 8, 128), f32),
            pltpu.VMEM((8, 128), f32),
            pltpu.SMEM((channels,), jnp.int32),
            dma((4,)),
            dma((1 + halves,)),
            dma((1 + halves,)),
            dma((2,)),
            dma((2,)),
            dma((2, halos)),
            dma((2, halos)),
            dma((2, halves)),
            dma((2, halves)),
            dma((2, MATVECS)),
            dma((2, MATVECS)),
            dma((MATVECS + 1,)),
            dma((MATVECS + 1,)),
            dma((1 + tiles,)),
        ],
        compiler_params=pltpu.CompilerParams(
            collective_id=0, has_side_effects=True, vmem_limit_bytes=60 * 1024 * 1024
        ),
    )(
        channel_charge, sector_dims[0, 0], left_env[0, 0], right_env[0, 0],
        left_block[0, 0], right_block[0, 0], inv_sv[0], precond[0, 0],
    )
    following, image, projected = pl.pallas_call(
        finish, name="finish", out_shape=out_shape,
        in_specs=[vmem] * 3, out_specs=(vmem, vmem, vmem),
    )(*results)
    return following[None, None], image[None, None], projected[None]


def solution(mesh):
    in_specs = (
        P("seg", "sec", None, None, None),
        P("seg", "sec", None, None, None),
        P("seg", "sec", None, None),
        P("seg", "sec", None, None),
        P("seg", "sec", None),
        P("seg", "sec", None, None),
        P("seg", "sec", None),
        P(),
    )
    out_specs = (P("seg", "sec", None, None), P("seg", "sec", None, None), P("seg", None, None))
    return jax.shard_map(
        per_device, mesh=mesh, in_specs=in_specs, out_specs=out_specs, check_vma=False
    )
```

```python
import functools

import jax
import jax.numpy as jnp
from jax import lax
from jax.experimental import pallas as pl
from jax.experimental.pallas import tpu as pltpu
from jax.sharding import PartitionSpec as P

MATVECS = 4
EPS = 1e-06
ROWS = 256
COLS = 256
CHUNK = 32
NORM = 3 * MATVECS
MESH = pl.DeviceIdType.MESH


def fold(values):
    rows, columns = values.shape
    block = jnp.sum(values.reshape(rows // 8, 8, columns), axis=0)
    total = block[:, :128]
    for at in range(128, columns, 128):
        total = total + block[:, at : at + 128]
    return total


def spread(tile, rows, columns):
    wide = jnp.concatenate([tile] * (columns // 128), axis=1)
    return jnp.concatenate([wide] * (rows // 8), axis=0)


def kernel(
    segs, secs,
    charge_ref, dims_ref, left_hbm, right_hbm, block_hbm, other_hbm, inv_ref, precond_hbm,
    next_hbm, image_hbm, projected_ref,
    left_ref, right_ref, block_ref, pinv_ref, nb_ref, ninv_ref, scaled_ref, basis_ref,
    up_basis, low_basis, edge_pinv, up_pinv, low_pinv, lx_ref, prefix_ref,
    stay_ref, up_out, low_out, up_in, low_in, image_ref, remain_ref, following_ref,
    slots_ref, norm_ref, late_ref, own_ref, early_ref, cross_ref, scale_ref, proj_ref, order_ref,
    load_sem, guess_send, guess_recv, pinv_send, pinv_recv, halo_send, halo_recv,
    first_send, first_recv, edge_send, edge_recv, sum_send, sum_recv, store_sem,
):
    channels, width, _ = left_ref.shape
    tiles = width // ROWS
    halves = width // COLS
    pieces = tiles * halves
    edge = width - ROWS
    count = secs * width * width
    f32, bf16 = jnp.float32, jnp.bfloat16
    seg, sec = lax.axis_index("seg"), lax.axis_index("sec")
    seg_before = lax.rem(seg + segs - 1, segs)
    seg_after = lax.rem(seg + 1, segs)
    above = (seg, lax.rem(sec + 1, secs))
    below = (seg, lax.rem(sec + secs - 1, secs))
    has_above = sec < secs - 1
    has_below = sec > 0
    edge_rows = pl.ds(edge, ROWS)

    load_left = pltpu.make_async_copy(left_hbm, left_ref, load_sem.at[0])
    load_right = pltpu.make_async_copy(right_hbm, right_ref, load_sem.at[1])
    load_block = pltpu.make_async_copy(block_hbm, block_ref, load_sem.at[2])
    load_precond = pltpu.make_async_copy(precond_hbm, pinv_ref, load_sem.at[3])
    load_precond.start()
    load_block.start()
    load_left.start()
    load_right.start()

    barrier = pltpu.get_barrier_semaphore()
    pl.semaphore_signal(barrier, inc=1, device_id=(seg_before, sec), device_id_type=MESH)
    pl.semaphore_signal(barrier, inc=1, device_id=(seg_after, sec), device_id_type=MESH)
    for offset in range(1, secs):
        peer = lax.rem(sec + offset, secs)
        pl.semaphore_signal(barrier, inc=1, device_id=(seg, peer), device_id_type=MESH)
    pl.semaphore_wait(barrier, secs + 1)

    def remote(src, dst, send, recv, device):
        return pltpu.make_async_remote_copy(
            src_ref=src, dst_ref=dst, send_sem=send, recv_sem=recv,
            device_id=device, device_id_type=MESH,
        )

    send_inv = remote(
        inv_ref, ninv_ref, guess_send.at[0], guess_recv.at[0], (seg_before, sec)
    )

    def send_block(h):
        across = pl.ds(h * COLS, COLS)
        return remote(
            other_hbm.at[:, across], nb_ref.at[:, across],
            guess_send.at[h + 1], guess_recv.at[h + 1], (seg_before, sec),
        )

    send_inv.start()
    for h in range(halves):
        send_block(h).start()

    to_above = remote(edge_pinv, low_pinv, pinv_send.at[0], pinv_recv.at[0], above)
    to_below = remote(edge_pinv, up_pinv, pinv_send.at[1], pinv_recv.at[1], below)

    def first_above(h):
        across = pl.ds(h * COLS, COLS)
        return remote(
            basis_ref.at[0, edge_rows, across], low_basis.at[0, :, across],
            first_send.at[0, h], first_recv.at[0, h], above,
        )

    def first_below(h):
        across = pl.ds(h * COLS, COLS)
        return remote(
            basis_ref.at[0, edge_rows, across], up_basis.at[0, :, across],
            first_send.at[1, h], first_recv.at[1, h], below,
        )

    def basis_above(k):
        return remote(
            basis_ref.at[k, edge_rows, :], low_basis.at[k],
            edge_send.at[0, k], edge_recv.at[0, k], above,
        )

    def basis_below(k):
        return remote(
            basis_ref.at[k, edge_rows, :], up_basis.at[k],
            edge_send.at[1, k], edge_recv.at[1, k], below,
        )

    def up_copy(n):
        return remote(
            up_out.at[n], up_in.at[n], halo_send.at[0, n], halo_recv.at[0, n], above
        )

    def low_copy(n):
        return remote(
            low_out.at[n], low_in.at[n], halo_send.at[1, n], halo_recv.at[1, n], below
        )

    keys = []
    for w in range(channels):
        q = charge_ref[w]
        keys.append(jnp.where(q == 1, 0, jnp.where(q == -1, 1, 2)))
    raising = jnp.int32(0)
    moving = jnp.int32(0)
    for w in range(channels):
        raising = raising + jnp.where(keys[w] == 0, 1, 0)
        moving = moving + jnp.where(keys[w] <= 1, 1, 0)
    places = []
    for w in range(channels):
        place = jnp.int32(0)
        for v in range(channels):
            if v < w:
                place = place + jnp.where(keys[v] <= keys[w], 1, 0)
            elif v > w:
                place = place + jnp.where(keys[v] < keys[w], 1, 0)
        places.append(place)
    for i in range(channels):
        who = jnp.int32(0)
        for w in range(channels):
            who = who + jnp.where(places[w] == i, w, 0)
        order_ref[i] = who

    proj_ref[...] = jnp.zeros_like(proj_ref)

    def chunked(rows, body):
        @pl.loop(0, rows // CHUNK)
        def _(c):
            body(pl.ds(pl.multiple_of(c * CHUNK, CHUNK), CHUNK))

    def clear(at):
        for k in range(1, MATVECS):
            basis_ref[k, at, :] = jnp.zeros((CHUNK, width), bf16)

    def clear_prefix(at):
        prefix_ref[0, at, :] = jnp.zeros((CHUNK, COLS), f32)

    def clear_edges(at):
        for k in range(1, MATVECS):
            up_basis[k, at, :] = jnp.zeros((CHUNK, width), bf16)
            low_basis[k, at, :] = jnp.zeros((CHUNK, width), bf16)

    chunked(width, clear)
    chunked(ROWS, clear_edges)
    chunked(ROWS, clear_prefix)

    def no_neighbour(halo, vectors, inverse):
        @pl.loop(0, MATVECS * pieces)
        def _(n):
            halo[n] = jnp.zeros((ROWS, COLS), bf16)

        vectors[0] = jnp.zeros((ROWS, width), bf16)
        inverse[...] = jnp.ones((ROWS, width), bf16)

    pl.when(sec == 0)(lambda: no_neighbour(up_in, low_basis, low_pinv))
    pl.when(sec == secs - 1)(lambda: no_neighbour(low_in, up_basis, up_pinv))

    def masked(values, start, left=0):
        row = start + lax.broadcasted_iota(jnp.int32, values.shape, 0)
        column = left + lax.broadcasted_iota(jnp.int32, values.shape, 1)
        inside = (row < dims_ref[0]) & (column < dims_ref[1])
        return jnp.where(inside, values, 0.0)

    load_precond.wait()

    @pl.loop(0, width // CHUNK)
    def _(c):
        at = pl.ds(pl.multiple_of(c * CHUNK, CHUNK), CHUNK)
        pinv_ref[at, :] = masked(1.0 / pinv_ref[at, :], c * CHUNK)

    @pl.loop(0, ROWS // CHUNK)
    def _(c):
        at = pl.ds(pl.multiple_of(edge + c * CHUNK, CHUNK), CHUNK)
        inner = pl.ds(pl.multiple_of(c * CHUNK, CHUNK), CHUNK)
        edge_pinv[inner, :] = pinv_ref[at, :].astype(bf16)

    pl.when(has_above)(lambda: to_above.start())
    pl.when(has_below)(lambda: to_below.start())

    lane = lax.broadcasted_iota(jnp.int32, (8, 128), 1)
    line = lax.broadcasted_iota(jnp.int32, (8, 128), 0)
    zero = jnp.zeros((8, 128), f32)

    def sum_copies(r):
        own = slots_ref.at[r, sec]
        return [
            remote(
                own, own, sum_send.at[r], sum_recv.at[r],
                (seg, lax.rem(sec + offset, secs)),
            )
            for offset in range(1, secs)
        ]

    def publish(r, parts):
        tile = zero
        for at, part in parts.items():
            tile = jnp.where(lane == at, jnp.sum(part, axis=1, keepdims=True), tile)
        slots_ref[r, sec] = jnp.sum(tile, axis=0, keepdims=True)
        for copy in sum_copies(r):
            copy.start()

    def collect(r):
        arrived = slots_ref.at[r, pl.ds(0, secs - 1)]
        pltpu.make_async_copy(arrived, arrived, sum_recv.at[r]).wait()
        total = jnp.sum(slots_ref[r], axis=0) * (1.0 / count)
        total = jnp.broadcast_to(total, (8, 128))

        def entry(at):
            value = jnp.sum(jnp.where(lane == at, total, 0.0), axis=1, keepdims=True)
            return jnp.broadcast_to(value, (8, 128))

        return entry

    def left_part(k, t, h):
        rows, across = pl.ds(t * ROWS, ROWS), pl.ds(h * COLS, COLS)
        vector = basis_ref[k, :, across]
        for w in range(channels):
            lx_ref[w, rows, across] = jnp.dot(
                left_ref[w, rows, :], vector, preferred_element_type=f32
            ).astype(bf16)

    send_inv.wait_recv()
    load_block.wait()
    scaled_ref[...] = (
        block_ref[...].astype(f32) * ninv_ref[...].astype(f32)
    ).astype(bf16)

    for h in range(halves):
        across = pl.ds(h * COLS, COLS)
        send_block(h).wait_recv()
        for t in range(tiles):
            rows = pl.ds(t * ROWS, ROWS)
            guess = masked(
                jnp.dot(
                    scaled_ref[rows, :], nb_ref[:, across], preferred_element_type=f32
                ),
                t * ROWS, h * COLS,
            )
            basis_ref[0, rows, across] = guess.astype(bf16)
        pl.when(has_above)(lambda: first_above(h).start())
        pl.when(has_below)(lambda: first_below(h).start())
        if h == 0:
            load_left.wait()
        if h < halves - 1:
            for t in range(tiles):
                left_part(0, t, h)
        if h == 0:
            @pl.when(has_below)
            def _():
                to_above.wait_recv()

            @pl.when(has_above)
            def _():
                to_below.wait_recv()

            load_right.wait()

    def edge_sums(k, h, c, some):
        n = k * pieces + (tiles - 1) * halves + h
        across = pl.ds(h * COLS, COLS)
        if isinstance(c, int):
            inner, at = pl.ds(c * CHUNK, CHUNK), pl.ds(edge + c * CHUNK, CHUNK)
        else:
            inner = pl.ds(pl.multiple_of(c * CHUNK, CHUNK), CHUNK)
            at = pl.ds(pl.multiple_of(edge + c * CHUNK, CHUNK), CHUNK)
        stay = stay_ref[at, across]
        up = up_out[n, inner, :].astype(f32)
        low = low_out[n, inner, :].astype(f32)

        def three(j):
            return basis_ref[j, at, across], up_basis[j, inner, across], low_basis[j, inner, across]

        mine, over, under = [vector.astype(f32) for vector in three(k)]
        sums = [fold(mine * stay + over * up + under * low)]
        stay = (stay * pinv_ref[at, across]).astype(bf16)
        up = up_out[n, inner, :] * up_pinv[inner, across]
        low = low_out[n, inner, :] * low_pinv[inner, across]
        for j in some:
            mine, over, under = three(j)
            sums.append(fold((mine * stay + over * up + under * low).astype(f32)))
        return sums

    def edge_arrived(k):
        @pl.when(has_below)
        def _():
            basis_above(k).wait_recv()

        @pl.when(has_above)
        def _():
            basis_below(k).wait_recv()

    def first_arrived():
        for h in range(halves):
            @pl.when(has_below)
            def _():
                first_above(h).wait_recv()

            @pl.when(has_above)
            def _():
                first_below(h).wait_recv()

    def portion(i, total):
        return range(i * total // channels, (i + 1) * total // channels)

    def product(k, first=False):
        own = [zero] * (MATVECS + 1)
        early = [zero] * (MATVECS + 1)
        for t in range(tiles):
            rows = pl.ds(t * ROWS, ROWS)
            for h in range(halves - 1 if first else 0, halves):
                left_part(k, t, h)
            for h in range(halves):
                n = k * pieces + t * halves + h
                across = pl.ds(h * COLS, COLS)
                for i in range(channels):
                    w = order_ref[i]
                    term = lax.dot_general(
                        lx_ref[w, rows, :], right_ref[w, across, :], (((1,), (1,)), ((), ())),
                        preferred_element_type=f32,
                    )
                    prefix_ref[i + 1] = prefix_ref[i] + term
                    if t == 0:
                        share = width // CHUNK // halves
                        for c in portion(i, share):
                            at = pl.ds((h * share + c) * CHUNK, CHUNK)
                            current = basis_ref[k, at, :].astype(f32)
                            lifted = current * pinv_ref[at, :]
                            for j in range(MATVECS):
                                vector = basis_ref[j, at, :].astype(f32)
                                own[j] = own[j] + fold(vector * lifted)
                            own[MATVECS] = own[MATVECS] + fold(current * current)
                    if t == tiles - 1 and h > 0:
                        for c in portion(i, ROWS // CHUNK):
                            sums = edge_sums(k, h - 1, c, range(MATVECS))
                            early = [a + b for a, b in zip(early, sums)]
                first_sum = prefix_ref[raising]
                second_sum = prefix_ref[moving]
                up_out[n] = first_sum.astype(bf16)
                low_out[n] = (second_sum - first_sum).astype(bf16)
                pl.when(has_above)(lambda: up_copy(n).start())
                pl.when(has_below)(lambda: low_copy(n).start())
                stay_ref[rows, across] = prefix_ref[channels] - second_sum
                if t == tiles - 1 and h == 0:
                    if first:
                        first_arrived()
                    else:
                        edge_arrived(k)
        for j in range(MATVECS + 1):
            own_ref[j] = own[j]
            early_ref[j] = early[j]

    product(0, True)

    @pl.loop(0, MATVECS)
    def _(k):
        def gather(piece):
            n = k * pieces + piece

            @pl.when(has_below)
            def _():
                up_copy(n).wait_recv()

            @pl.when(has_above)
            def _():
                low_copy(n).wait_recv()

        def arrived(piece, c):
            t, h = divmod(piece, halves)
            n = k * pieces + piece
            across = pl.ds(h * COLS, COLS)
            inner = pl.ds(pl.multiple_of(c * CHUNK, CHUNK), CHUNK)
            start = t * ROWS + c * CHUNK
            at = pl.ds(pl.multiple_of(start, CHUNK), CHUNK)
            image = stay_ref[at, across] + up_in[n, inner, :].astype(f32)
            image = image + low_in[n, inner, :].astype(f32)
            image_ref[at, across] = image
            return at, across, image

        def finish_step(kk):
            some = range(kk + 1)
            past = range(kk)

            def add(carry, new):
                return tuple(a + b for a, b in zip(carry, new))

            def sent(c, carry):
                return add(carry, edge_sums(kk, halves - 1, c, some))

            carry = tuple(early_ref[j] for j in range(kk + 2))
            carry = lax.fori_loop(0, ROWS // CHUNK, sent, carry)

            def received(piece):
                def body(c, carry):
                    at, across, image = arrived(piece, c)
                    lifted = image * pinv_ref[at, across]
                    vectors = [basis_ref[j, at, across].astype(f32) for j in some]
                    new = [fold(vectors[kk] * image)]
                    new += [fold(vector * lifted) for vector in vectors]
                    return add(carry, new)

                return body

            for piece in range(pieces - halves):
                gather(piece)
                carry = lax.fori_loop(0, ROWS // CHUNK, received(piece), carry)

            parts = {0: carry[0], NORM: own_ref[MATVECS]}
            for j in some:
                parts[MATVECS + j] = carry[1 + j]
                parts[2 * MATVECS + j] = own_ref[j]
            for j in range(kk - 1):
                parts[NORM + 1 + j] = cross_ref[j]
            publish(kk, parts)

            final = kk == MATVECS - 1

            def crossed(at, across, image):
                vectors = [basis_ref[j, at, across].astype(f32) for j in past]
                new = [fold(vector * image) for vector in vectors]
                if final:
                    pinv = pinv_ref[at, across]
                    current = basis_ref[kk, at, across].astype(f32)
                    lifted, current_lifted = image * pinv, current * pinv
                    new.append(fold(lifted * lifted))
                    new.append(fold(lifted * current_lifted))
                    new.append(fold(current_lifted * current_lifted))
                return new

            def gram_sums(c, carry):
                at = pl.ds(pl.multiple_of(c * CHUNK, CHUNK), CHUNK)
                vectors = [basis_ref[j, at, :].astype(f32) for j in some]
                return add(carry, [fold(vectors[i] * vectors[j]) for i, j in pairs])

            def resting(c, carry):
                at = pl.ds(pl.multiple_of(c * CHUNK, CHUNK), CHUNK)
                for h in range(halves):
                    across = pl.ds(h * COLS, COLS)
                    carry = add(carry, crossed(at, across, image_ref[at, across]))
                return carry

            pairs = [(i, j) for i in some for j in range(i + 1)] if final else []
            gram = (zero,) * len(pairs)
            cross = (zero,) * (kk + 3 if final else kk)
            if final:
                gram = lax.fori_loop(0, width // CHUNK, gram_sums, gram)
            if kk:
                cross = lax.fori_loop(0, edge // CHUNK, resting, cross)

            for piece in range(pieces - halves, pieces):
                gather(piece)

                def land(c, carry):
                    at, across, image = arrived(piece, c)
                    return add(carry, crossed(at, across, image))

                cross = lax.fori_loop(0, ROWS // CHUNK, land, cross)

            if final:
                publish(MATVECS, dict(enumerate(cross + gram)))

            entry = collect(kk)
            scale = lax.rsqrt(entry(NORM) + EPS)
            scales = [scale_ref[j] for j in past] + [scale]
            diagonal = scale * scale * entry(0)
            drop = scale * diagonal
            coefficients = [
                scales[j] * scales[j] * scale
                * (entry(MATVECS + j) - diagonal * entry(2 * MATVECS + j))
                for j in some
            ]

            def update(c, carry):
                at = pl.ds(pl.multiple_of(c * CHUNK, CHUNK), CHUNK)
                for h in range(halves):
                    across = pl.ds(h * COLS, COLS)

                    def wide(tile):
                        return spread(tile, CHUNK, COLS)

                    image = image_ref[at, across] * wide(scale)
                    if kk == MATVECS - 1:
                        image_ref[at, across] = masked(image, c * CHUNK, h * COLS)
                    vectors = [basis_ref[j, at, across].astype(f32) for j in some]
                    remain = (image - wide(drop) * vectors[kk]) * pinv_ref[at, across]
                    for j in some:
                        remain = remain - wide(coefficients[j]) * vectors[j]
                    if final:
                        remain_ref[at, across] = remain
                    else:
                        basis_ref[kk + 1, at, across] = remain.astype(bf16)
                return carry

            lax.fori_loop(edge // CHUNK, width // CHUNK, update, 0)
            if kk < MATVECS - 1:
                pl.when(has_above)(lambda: basis_above(kk + 1).start())
                pl.when(has_below)(lambda: basis_below(kk + 1).start())
            lax.fori_loop(0, edge // CHUNK, update, 0)
            scale_ref[kk] = scale
            if not final:
                for j in past:
                    cross_ref[j] = cross[j]
            proj = jnp.where((line == kk) & (lane == kk), diagonal, proj_ref[...])
            for j in range(kk - 1):
                value = scales[j] * scales[kk - 1] * entry(NORM + 1 + j)
                proj = jnp.where((line == j) & (lane == kk - 1), value, proj)
            proj_ref[...] = proj
            if final:
                late_ref[0] = scale
                late_ref[1] = drop
                mixed = zero
                for j in some:
                    late_ref[2 + j] = coefficients[j]
                    mixed = mixed + 2.0 * coefficients[j] * (
                        drop * entry(2 * MATVECS + j) - scale * entry(MATVECS + j)
                    )
                norm_ref[...] = mixed

        for kk in range(MATVECS):
            pl.when(k == kk)(functools.partial(finish_step, kk))
        pl.when(k < MATVECS - 1)(lambda: product(k + 1))

    last = MATVECS - 1
    store_image = pltpu.make_async_copy(image_ref, image_hbm, store_sem.at[0])
    store_image.start()

    send_inv.wait_send()
    for h in range(halves):
        send_block(h).wait_send()

    @pl.when(has_above)
    def _():
        to_above.wait_send()

        @pl.loop(0, MATVECS * pieces)
        def _(n):
            up_copy(n).wait_send()

        for h in range(halves):
            first_above(h).wait_send()

        @pl.loop(1, MATVECS)
        def _(k):
            basis_above(k).wait_send()

    @pl.when(has_below)
    def _():
        to_below.wait_send()

        @pl.loop(0, MATVECS * pieces)
        def _(n):
            low_copy(n).wait_send()

        for h in range(halves):
            first_below(h).wait_send()

        @pl.loop(1, MATVECS)
        def _(k):
            basis_below(k).wait_send()

    entry = collect(MATVECS)
    scale, drop = late_ref[0], late_ref[1]
    square = norm_ref[...] + scale * scale * entry(last) + drop * drop * entry(last + 2)
    square = square - 2.0 * scale * drop * entry(last + 1)
    at = last + 3
    for i in range(MATVECS):
        for j in range(i + 1):
            twice = 1.0 if i == j else 2.0
            square = square + twice * late_ref[2 + i] * late_ref[2 + j] * entry(at)
            at += 1
    scale = lax.rsqrt(jnp.maximum(square, 0.0) + EPS)

    def store(t):
        rows = pl.ds(t * ROWS, ROWS)
        return pltpu.make_async_copy(
            following_ref.at[rows, :], next_hbm.at[rows, :], store_sem.at[1 + t]
        )

    for t in range(tiles):
        @pl.loop(t * ROWS // CHUNK, (t + 1) * ROWS // CHUNK)
        def _(c):
            at = pl.ds(pl.multiple_of(c * CHUNK, CHUNK), CHUNK)
            following_ref[at, :] = (
                remain_ref[at, :] * spread(scale, CHUNK, width)
            ).astype(bf16)

        store(t).start()

    proj = proj_ref[...]
    for j in range(last):
        value = scale_ref[j] * scale_ref[last] * entry(j)
        proj = jnp.where((line == j) & (lane == last), value, proj)
    projected_ref[...] = proj[:MATVECS, :MATVECS]

    @pl.loop(0, MATVECS + 1)
    def _(r):
        sent = slots_ref.at[r, pl.ds(0, secs - 1)]
        pltpu.make_async_copy(sent, sent, sum_send.at[r]).wait()

    store_image.wait()
    for t in range(tiles):
        store(t).wait()


def finish(next_in, image_in, projected_in, next_ref, image_ref, projected_ref):
    next_ref[...] = next_in[...]
    image_ref[...] = image_in[...]
    projected_ref[...] = projected_in[...]


def per_device(
    left_env, right_env, left_block, right_block, inv_sv, precond, sector_dims, channel_charge
):
    segs, secs = lax.axis_size("seg"), lax.axis_size("sec")
    channels, width = left_env.shape[2], left_env.shape[-1]
    tiles, halves = width // ROWS, width // COLS
    halos = MATVECS * tiles * halves
    f32, bf16 = jnp.float32, jnp.bfloat16
    vmem = pl.BlockSpec(memory_space=pltpu.VMEM)
    smem = pl.BlockSpec(memory_space=pltpu.SMEM)
    hbm = pl.BlockSpec(memory_space=pl.ANY)
    out_shape = (
        jax.ShapeDtypeStruct((width, width), bf16),
        jax.ShapeDtypeStruct((width, width), f32),
        jax.ShapeDtypeStruct((MATVECS, MATVECS), f32),
    )
    dma = pltpu.SemaphoreType.DMA
    results = pl.pallas_call(
        functools.partial(kernel, segs, secs),
        name="davidson",
        out_shape=out_shape,
        in_specs=[smem, smem, hbm, hbm, hbm, hbm, vmem, hbm],
        out_specs=(hbm, hbm, vmem),
        scratch_shapes=[
            pltpu.VMEM((channels, width, width), bf16),
            pltpu.VMEM((channels, width, width), bf16),
            pltpu.VMEM((width, width), bf16),
            pltpu.VMEM((width, width), f32),
            pltpu.VMEM((width, width), bf16),
            pltpu.VMEM((1, width), bf16),
            pltpu.VMEM((width, width), bf16),
            pltpu.VMEM((MATVECS, width, width), bf16),
            pltpu.VMEM((MATVECS, ROWS, width), bf16),
            pltpu.VMEM((MATVECS, ROWS, width), bf16),
            pltpu.VMEM((ROWS, width), bf16),
            pltpu.VMEM((ROWS, width), bf16),
            pltpu.VMEM((ROWS, width), bf16),
            pltpu.VMEM((channels, width, width), bf16),
            pltpu.VMEM((channels + 1, ROWS, COLS), f32),
            pltpu.VMEM((width, width), f32),
            pltpu.VMEM((halos, ROWS, COLS), bf16),
            pltpu.VMEM((halos, ROWS, COLS), bf16),
            pltpu.VMEM((halos, ROWS, COLS), bf16),
            pltpu.VMEM((halos, ROWS, COLS), bf16),
            pltpu.VMEM((width, width), f32),
            pltpu.VMEM((width, width), f32),
            pltpu.VMEM((width, width), bf16),
            pltpu.VMEM((MATVECS + 1, secs, 1, 128), f32),
            pltpu.VMEM((8, 128), f32),
            pltpu.VMEM((MATVECS + 2, 8, 128), f32),
            pltpu.VMEM((MATVECS + 1, 8, 128), f32),
            pltpu.VMEM((MATVECS + 1, 8, 128), f32),
            pltpu.VMEM((MATVECS, 8, 128), f32),
            pltpu.VMEM((MATVECS, 8, 128), f32),
            pltpu.VMEM((8, 128), f32),
            pltpu.SMEM((channels,), jnp.int32),
            dma((4,)),
            dma((1 + halves,)),
            dma((1 + halves,)),
            dma((2,)),
            dma((2,)),
            dma((2, halos)),
            dma((2, halos)),
            dma((2, halves)),
            dma((2, halves)),
            dma((2, MATVECS)),
            dma((2, MATVECS)),
            dma((MATVECS + 1,)),
            dma((MATVECS + 1,)),
            dma((1 + tiles,)),
        ],
        compiler_params=pltpu.CompilerParams(
            collective_id=0, has_side_effects=True, vmem_limit_bytes=60 * 1024 * 1024
        ),
    )(
        channel_charge, sector_dims[0, 0], left_env[0, 0], right_env[0, 0],
        left_block[0, 0], right_block[0, 0], inv_sv[0], precond[0, 0],
    )
    following, image, projected = pl.pallas_call(
        finish, name="finish", out_shape=out_shape,
        in_specs=[vmem] * 3, out_specs=(vmem, vmem, vmem),
    )(*results)
    return following[None, None], image[None, None], projected[None]


def solution(mesh):
    in_specs = (
        P("seg", "sec", None, None, None),
        P("seg", "sec", None, None, None),
        P("seg", "sec", None, None),
        P("seg", "sec", None, None),
        P("seg", "sec", None),
        P("seg", "sec", None, None),
        P("seg", "sec", None),
        P(),
    )
    out_specs = (P("seg", "sec", None, None), P("seg", "sec", None, None), P("seg", None, None))
    return jax.shard_map(
        per_device, mesh=mesh, in_specs=in_specs, out_specs=out_specs, check_vma=False
    )
```

```python
import functools

import jax
import jax.numpy as jnp
from jax import lax
from jax.experimental import pallas as pl
from jax.experimental.pallas import tpu as pltpu
from jax.sharding import PartitionSpec as P

MATVECS = 4
EPS = 1e-06
ROWS = 256
COLS = 256
CHUNK = 64
NORM = 3 * MATVECS
MESH = pl.DeviceIdType.MESH


def fold(values):
    rows, columns = values.shape
    block = jnp.sum(values.reshape(rows // 8, 8, columns), axis=0)
    total = block[:, :128]
    for at in range(128, columns, 128):
        total = total + block[:, at : at + 128]
    return total


def spread(tile, rows, columns):
    wide = jnp.concatenate([tile] * (columns // 128), axis=1)
    return jnp.concatenate([wide] * (rows // 8), axis=0)


def kernel(
    segs, secs,
    charge_ref, dims_ref, left_hbm, right_hbm, block_hbm, other_hbm, inv_ref, precond_hbm,
    next_hbm, image_hbm, projected_ref,
    left_ref, right_ref, block_ref, pinv_ref, nb_ref, ninv_ref, scaled_ref, basis_ref,
    up_basis, low_basis, edge_pinv, up_pinv, low_pinv, lx_ref, prefix_ref,
    stay_ref, up_out, low_out, up_in, low_in, image_ref, remain_ref, following_ref,
    slots_ref, norm_ref, late_ref, own_ref, early_ref, cross_ref, scale_ref, proj_ref, order_ref,
    load_sem, guess_send, guess_recv, pinv_send, pinv_recv, halo_send, halo_recv,
    first_send, first_recv, edge_send, edge_recv, sum_send, sum_recv, store_sem,
):
    channels, width, _ = left_ref.shape
    tiles = width // ROWS
    halves = width // COLS
    pieces = tiles * halves
    edge = width - ROWS
    count = secs * width * width
    f32, bf16 = jnp.float32, jnp.bfloat16
    seg, sec = lax.axis_index("seg"), lax.axis_index("sec")
    seg_before = lax.rem(seg + segs - 1, segs)
    seg_after = lax.rem(seg + 1, segs)
    above = (seg, lax.rem(sec + 1, secs))
    below = (seg, lax.rem(sec + secs - 1, secs))
    has_above = sec < secs - 1
    has_below = sec > 0
    edge_rows = pl.ds(edge, ROWS)

    load_left = pltpu.make_async_copy(left_hbm, left_ref, load_sem.at[0])
    load_right = pltpu.make_async_copy(right_hbm, right_ref, load_sem.at[1])
    load_block = pltpu.make_async_copy(block_hbm, block_ref, load_sem.at[2])
    load_precond = pltpu.make_async_copy(precond_hbm, pinv_ref, load_sem.at[3])
    load_precond.start()
    load_block.start()
    load_left.start()
    load_right.start()

    barrier = pltpu.get_barrier_semaphore()
    pl.semaphore_signal(barrier, inc=1, device_id=(seg_after, sec), device_id_type=MESH)
    for offset in range(1, secs):
        peer = lax.rem(sec + offset, secs)
        pl.semaphore_signal(barrier, inc=1, device_id=(seg, peer), device_id_type=MESH)
    pl.semaphore_wait(barrier, secs)

    def remote(src, dst, send, recv, device):
        return pltpu.make_async_remote_copy(
            src_ref=src, dst_ref=dst, send_sem=send, recv_sem=recv,
            device_id=device, device_id_type=MESH,
        )

    send_inv = remote(
        inv_ref, ninv_ref, guess_send.at[0], guess_recv.at[0], (seg_before, sec)
    )

    def send_block(h):
        across = pl.ds(h * COLS, COLS)
        return remote(
            other_hbm.at[:, across], nb_ref.at[:, across],
            guess_send.at[h + 1], guess_recv.at[h + 1], (seg_before, sec),
        )

    send_inv.start()
    for h in range(halves):
        send_block(h).start()

    to_above = remote(edge_pinv, low_pinv, pinv_send.at[0], pinv_recv.at[0], above)
    to_below = remote(edge_pinv, up_pinv, pinv_send.at[1], pinv_recv.at[1], below)

    def first_above(h):
        across = pl.ds(h * COLS, COLS)
        return remote(
            basis_ref.at[0, edge_rows, across], low_basis.at[0, :, across],
            first_send.at[0, h], first_recv.at[0, h], above,
        )

    def first_below(h):
        across = pl.ds(h * COLS, COLS)
        return remote(
            basis_ref.at[0, edge_rows, across], up_basis.at[0, :, across],
            first_send.at[1, h], first_recv.at[1, h], below,
        )

    def basis_above(k):
        return remote(
            basis_ref.at[k, edge_rows, :], low_basis.at[k],
            edge_send.at[0, k], edge_recv.at[0, k], above,
        )

    def basis_below(k):
        return remote(
            basis_ref.at[k, edge_rows, :], up_basis.at[k],
            edge_send.at[1, k], edge_recv.at[1, k], below,
        )

    def up_copy(n):
        return remote(
            up_out.at[n], up_in.at[n], halo_send.at[0, n], halo_recv.at[0, n], above
        )

    def low_copy(n):
        return remote(
            low_out.at[n], low_in.at[n], halo_send.at[1, n], halo_recv.at[1, n], below
        )

    keys = []
    for w in range(channels):
        q = charge_ref[w]
        keys.append(jnp.where(q == 1, 0, jnp.where(q == -1, 1, 2)))
    raising = jnp.int32(0)
    moving = jnp.int32(0)
    for w in range(channels):
        raising = raising + jnp.where(keys[w] == 0, 1, 0)
        moving = moving + jnp.where(keys[w] <= 1, 1, 0)
    places = []
    for w in range(channels):
        place = jnp.int32(0)
        for v in range(channels):
            if v < w:
                place = place + jnp.where(keys[v] <= keys[w], 1, 0)
            elif v > w:
                place = place + jnp.where(keys[v] < keys[w], 1, 0)
        places.append(place)
    for i in range(channels):
        who = jnp.int32(0)
        for w in range(channels):
            who = who + jnp.where(places[w] == i, w, 0)
        order_ref[i] = who

    proj_ref[...] = jnp.zeros_like(proj_ref)

    def chunked(rows, body):
        @pl.loop(0, rows // CHUNK)
        def _(c):
            body(pl.ds(pl.multiple_of(c * CHUNK, CHUNK), CHUNK))

    def clear(at):
        for k in range(1, MATVECS):
            basis_ref[k, at, :] = jnp.zeros((CHUNK, width), bf16)

    def clear_prefix(at):
        prefix_ref[0, at, :] = jnp.zeros((CHUNK, COLS), f32)

    def clear_edges(at):
        for k in range(1, MATVECS):
            up_basis[k, at, :] = jnp.zeros((CHUNK, width), bf16)
            low_basis[k, at, :] = jnp.zeros((CHUNK, width), bf16)

    chunked(width, clear)
    chunked(ROWS, clear_edges)
    chunked(ROWS, clear_prefix)

    def no_neighbour(halo, vectors, inverse):
        @pl.loop(0, MATVECS * pieces)
        def _(n):
            halo[n] = jnp.zeros((ROWS, COLS), bf16)

        vectors[0] = jnp.zeros((ROWS, width), bf16)
        inverse[...] = jnp.ones((ROWS, width), bf16)

    pl.when(sec == 0)(lambda: no_neighbour(up_in, low_basis, low_pinv))
    pl.when(sec == secs - 1)(lambda: no_neighbour(low_in, up_basis, up_pinv))

    def masked(values, start, left=0):
        row = start + lax.broadcasted_iota(jnp.int32, values.shape, 0)
        column = left + lax.broadcasted_iota(jnp.int32, values.shape, 1)
        inside = (row < dims_ref[0]) & (column < dims_ref[1])
        return jnp.where(inside, values, 0.0)

    load_precond.wait()

    @pl.loop(0, width // CHUNK)
    def _(c):
        at = pl.ds(pl.multiple_of(c * CHUNK, CHUNK), CHUNK)
        pinv_ref[at, :] = masked(1.0 / pinv_ref[at, :], c * CHUNK)

    @pl.loop(0, ROWS // CHUNK)
    def _(c):
        at = pl.ds(pl.multiple_of(edge + c * CHUNK, CHUNK), CHUNK)
        inner = pl.ds(pl.multiple_of(c * CHUNK, CHUNK), CHUNK)
        edge_pinv[inner, :] = pinv_ref[at, :].astype(bf16)

    pl.when(has_above)(lambda: to_above.start())
    pl.when(has_below)(lambda: to_below.start())

    lane = lax.broadcasted_iota(jnp.int32, (8, 128), 1)
    line = lax.broadcasted_iota(jnp.int32, (8, 128), 0)
    zero = jnp.zeros((8, 128), f32)

    def sum_copies(r):
        own = slots_ref.at[r, sec]
        return [
            remote(
                own, own, sum_send.at[r], sum_recv.at[r],
                (seg, lax.rem(sec + offset, secs)),
            )
            for offset in range(1, secs)
        ]

    def publish(r, parts):
        tile = zero
        for at, part in parts.items():
            tile = jnp.where(lane == at, jnp.sum(part, axis=1, keepdims=True), tile)
        slots_ref[r, sec] = jnp.sum(tile, axis=0, keepdims=True)
        for copy in sum_copies(r):
            copy.start()

    def collect(r):
        arrived = slots_ref.at[r, pl.ds(0, secs - 1)]
        pltpu.make_async_copy(arrived, arrived, sum_recv.at[r]).wait()
        total = jnp.sum(slots_ref[r], axis=0) * (1.0 / count)
        total = jnp.broadcast_to(total, (8, 128))

        def entry(at):
            value = jnp.sum(jnp.where(lane == at, total, 0.0), axis=1, keepdims=True)
            return jnp.broadcast_to(value, (8, 128))

        return entry

    def left_part(k, t, h):
        rows, across = pl.ds(t * ROWS, ROWS), pl.ds(h * COLS, COLS)
        vector = basis_ref[k, :, across]
        for w in range(channels):
            lx_ref[w, rows, across] = jnp.dot(
                left_ref[w, rows, :], vector, preferred_element_type=f32
            ).astype(bf16)

    send_inv.wait_recv()
    load_block.wait()
    scaled_ref[...] = (
        block_ref[...].astype(f32) * ninv_ref[...].astype(f32)
    ).astype(bf16)

    for h in range(halves):
        across = pl.ds(h * COLS, COLS)
        send_block(h).wait_recv()
        for t in range(tiles):
            rows = pl.ds(t * ROWS, ROWS)
            guess = masked(
                jnp.dot(
                    scaled_ref[rows, :], nb_ref[:, across], preferred_element_type=f32
                ),
                t * ROWS, h * COLS,
            )
            basis_ref[0, rows, across] = guess.astype(bf16)
        pl.when(has_above)(lambda: first_above(h).start())
        pl.when(has_below)(lambda: first_below(h).start())
        if h == 0:
            load_left.wait()
        if h < halves - 1:
            for t in range(tiles):
                left_part(0, t, h)
        if h == 0:
            @pl.when(has_below)
            def _():
                to_above.wait_recv()

            @pl.when(has_above)
            def _():
                to_below.wait_recv()

            load_right.wait()

    def edge_sums(k, h, c, some):
        n = k * pieces + (tiles - 1) * halves + h
        across = pl.ds(h * COLS, COLS)
        if isinstance(c, int):
            inner, at = pl.ds(c * CHUNK, CHUNK), pl.ds(edge + c * CHUNK, CHUNK)
        else:
            inner = pl.ds(pl.multiple_of(c * CHUNK, CHUNK), CHUNK)
            at = pl.ds(pl.multiple_of(edge + c * CHUNK, CHUNK), CHUNK)
        stay = stay_ref[at, across]
        up = up_out[n, inner, :].astype(f32)
        low = low_out[n, inner, :].astype(f32)

        def three(j):
            return basis_ref[j, at, across], up_basis[j, inner, across], low_basis[j, inner, across]

        mine, over, under = [vector.astype(f32) for vector in three(k)]
        sums = [fold(mine * stay + over * up + under * low)]
        stay = (stay * pinv_ref[at, across]).astype(bf16)
        up = up_out[n, inner, :] * up_pinv[inner, across]
        low = low_out[n, inner, :] * low_pinv[inner, across]
        for j in some:
            mine, over, under = three(j)
            sums.append(fold((mine * stay + over * up + under * low).astype(f32)))
        return sums

    def edge_arrived(k):
        @pl.when(has_below)
        def _():
            basis_above(k).wait_recv()

        @pl.when(has_above)
        def _():
            basis_below(k).wait_recv()

    def first_arrived():
        for h in range(halves):
            @pl.when(has_below)
            def _():
                first_above(h).wait_recv()

            @pl.when(has_above)
            def _():
                first_below(h).wait_recv()

    def portion(i, total):
        return range(i * total // channels, (i + 1) * total // channels)

    def product(k, first=False):
        own = [zero] * (MATVECS + 1)
        early = [zero] * (MATVECS + 1)
        for t in range(tiles):
            rows = pl.ds(t * ROWS, ROWS)
            for h in range(halves - 1 if first else 0, halves):
                left_part(k, t, h)
            for h in range(halves):
                n = k * pieces + t * halves + h
                across = pl.ds(h * COLS, COLS)
                for i in range(channels):
                    w = order_ref[i]
                    term = lax.dot_general(
                        lx_ref[w, rows, :], right_ref[w, across, :], (((1,), (1,)), ((), ())),
                        preferred_element_type=f32,
                    )
                    prefix_ref[i + 1] = prefix_ref[i] + term
                    if t == 0:
                        share = width // CHUNK // halves
                        for c in portion(i, share):
                            at = pl.ds((h * share + c) * CHUNK, CHUNK)
                            current = basis_ref[k, at, :].astype(f32)
                            lifted = current * pinv_ref[at, :]
                            for j in range(MATVECS):
                                vector = basis_ref[j, at, :].astype(f32)
                                own[j] = own[j] + fold(vector * lifted)
                            own[MATVECS] = own[MATVECS] + fold(current * current)
                    if t == tiles - 1 and h > 0:
                        for c in portion(i, ROWS // CHUNK):
                            sums = edge_sums(k, h - 1, c, range(MATVECS))
                            early = [a + b for a, b in zip(early, sums)]
                first_sum = prefix_ref[raising]
                second_sum = prefix_ref[moving]
                up_out[n] = first_sum.astype(bf16)
                low_out[n] = (second_sum - first_sum).astype(bf16)
                pl.when(has_above)(lambda: up_copy(n).start())
                pl.when(has_below)(lambda: low_copy(n).start())
                stay_ref[rows, across] = prefix_ref[channels] - second_sum
                if t == tiles - 1 and h == 0:
                    if first:
                        first_arrived()
                    else:
                        edge_arrived(k)
        for j in range(MATVECS + 1):
            own_ref[j] = own[j]
            early_ref[j] = early[j]

    product(0, True)

    @pl.loop(0, MATVECS)
    def _(k):
        def gather(piece):
            n = k * pieces + piece

            @pl.when(has_below)
            def _():
                up_copy(n).wait_recv()

            @pl.when(has_above)
            def _():
                low_copy(n).wait_recv()

        def arrived(piece, c):
            t, h = divmod(piece, halves)
            n = k * pieces + piece
            across = pl.ds(h * COLS, COLS)
            inner = pl.ds(pl.multiple_of(c * CHUNK, CHUNK), CHUNK)
            start = t * ROWS + c * CHUNK
            at = pl.ds(pl.multiple_of(start, CHUNK), CHUNK)
            image = stay_ref[at, across] + up_in[n, inner, :].astype(f32)
            image = image + low_in[n, inner, :].astype(f32)
            image_ref[at, across] = image
            return at, across, image

        def finish_step(kk):
            some = range(kk + 1)
            past = range(kk)

            def add(carry, new):
                return tuple(a + b for a, b in zip(carry, new))

            def sent(c, carry):
                return add(carry, edge_sums(kk, halves - 1, c, some))

            carry = tuple(early_ref[j] for j in range(kk + 2))
            carry = lax.fori_loop(0, ROWS // CHUNK, sent, carry)

            def received(piece):
                def body(c, carry):
                    at, across, image = arrived(piece, c)
                    lifted = image * pinv_ref[at, across]
                    lifted = lifted.astype(bf16)
                    new = [fold(basis_ref[kk, at, across].astype(f32) * image)]
                    new += [
                        fold((basis_ref[j, at, across] * lifted).astype(f32)) for j in some
                    ]
                    return add(carry, new)

                return body

            for piece in range(pieces - halves):
                gather(piece)
                carry = lax.fori_loop(0, ROWS // CHUNK, received(piece), carry)

            parts = {0: carry[0], NORM: own_ref[MATVECS]}
            for j in some:
                parts[MATVECS + j] = carry[1 + j]
                parts[2 * MATVECS + j] = own_ref[j]
            for j in range(kk - 1):
                parts[NORM + 1 + j] = cross_ref[j]
            publish(kk, parts)

            final = kk == MATVECS - 1

            def crossed(at, across, image):
                vectors = [basis_ref[j, at, across].astype(f32) for j in past]
                new = [fold(vector * image) for vector in vectors]
                if final:
                    pinv = pinv_ref[at, across]
                    current = basis_ref[kk, at, across].astype(f32)
                    lifted, current_lifted = image * pinv, current * pinv
                    new.append(fold(lifted * lifted))
                    new.append(fold(lifted * current_lifted))
                    new.append(fold(current_lifted * current_lifted))
                return new

            def gram_sums(c, carry):
                at = pl.ds(pl.multiple_of(c * CHUNK, CHUNK), CHUNK)
                vectors = [basis_ref[j, at, :].astype(f32) for j in some]
                return add(carry, [fold(vectors[i] * vectors[j]) for i, j in pairs])

            def resting(c, carry):
                at = pl.ds(pl.multiple_of(c * CHUNK, CHUNK), CHUNK)
                for h in range(halves):
                    across = pl.ds(h * COLS, COLS)
                    carry = add(carry, crossed(at, across, image_ref[at, across]))
                return carry

            pairs = [(i, j) for i in some for j in range(i + 1)] if final else []
            gram = (zero,) * len(pairs)
            cross = (zero,) * (kk + 3 if final else kk)
            if final:
                gram = lax.fori_loop(0, width // CHUNK, gram_sums, gram)
            if kk:
                cross = lax.fori_loop(0, edge // CHUNK, resting, cross)

            for piece in range(pieces - halves, pieces):
                gather(piece)

                def land(c, carry):
                    at, across, image = arrived(piece, c)
                    return add(carry, crossed(at, across, image))

                cross = lax.fori_loop(0, ROWS // CHUNK, land, cross)

            if final:
                publish(MATVECS, dict(enumerate(cross + gram)))

            entry = collect(kk)
            scale = lax.rsqrt(entry(NORM) + EPS)
            scales = [scale_ref[j] for j in past] + [scale]
            diagonal = scale * scale * entry(0)
            drop = scale * diagonal
            coefficients = [
                scales[j] * scales[j] * scale
                * (entry(MATVECS + j) - diagonal * entry(2 * MATVECS + j))
                for j in some
            ]

            def update(c, carry):
                at = pl.ds(pl.multiple_of(c * CHUNK, CHUNK), CHUNK)
                for h in range(halves):
                    across = pl.ds(h * COLS, COLS)

                    def wide(tile):
                        return spread(tile, CHUNK, COLS)

                    image = image_ref[at, across] * wide(scale)
                    if kk == MATVECS - 1:
                        image_ref[at, across] = masked(image, c * CHUNK, h * COLS)
                    vectors = [basis_ref[j, at, across].astype(f32) for j in some]
                    remain = (image - wide(drop) * vectors[kk]) * pinv_ref[at, across]
                    for j in some:
                        remain = remain - wide(coefficients[j]) * vectors[j]
                    if final:
                        remain_ref[at, across] = remain
                    else:
                        basis_ref[kk + 1, at, across] = remain.astype(bf16)
                return carry

            lax.fori_loop(edge // CHUNK, width // CHUNK, update, 0)
            if kk < MATVECS - 1:
                pl.when(has_above)(lambda: basis_above(kk + 1).start())
                pl.when(has_below)(lambda: basis_below(kk + 1).start())
            lax.fori_loop(0, edge // CHUNK, update, 0)
            scale_ref[kk] = scale
            if not final:
                for j in past:
                    cross_ref[j] = cross[j]
            proj = jnp.where((line == kk) & (lane == kk), diagonal, proj_ref[...])
            for j in range(kk - 1):
                value = scales[j] * scales[kk - 1] * entry(NORM + 1 + j)
                proj = jnp.where((line == j) & (lane == kk - 1), value, proj)
            proj_ref[...] = proj
            if final:
                late_ref[0] = scale
                late_ref[1] = drop
                mixed = zero
                for j in some:
                    late_ref[2 + j] = coefficients[j]
                    mixed = mixed + 2.0 * coefficients[j] * (
                        drop * entry(2 * MATVECS + j) - scale * entry(MATVECS + j)
                    )
                norm_ref[...] = mixed

        for kk in range(MATVECS):
            pl.when(k == kk)(functools.partial(finish_step, kk))
        pl.when(k < MATVECS - 1)(lambda: product(k + 1))

    last = MATVECS - 1
    store_image = pltpu.make_async_copy(image_ref, image_hbm, store_sem.at[0])
    store_image.start()

    send_inv.wait_send()
    for h in range(halves):
        send_block(h).wait_send()

    @pl.when(has_above)
    def _():
        to_above.wait_send()

        @pl.loop(0, MATVECS * pieces)
        def _(n):
            up_copy(n).wait_send()

        for h in range(halves):
            first_above(h).wait_send()

        @pl.loop(1, MATVECS)
        def _(k):
            basis_above(k).wait_send()

    @pl.when(has_below)
    def _():
        to_below.wait_send()

        @pl.loop(0, MATVECS * pieces)
        def _(n):
            low_copy(n).wait_send()

        for h in range(halves):
            first_below(h).wait_send()

        @pl.loop(1, MATVECS)
        def _(k):
            basis_below(k).wait_send()

    entry = collect(MATVECS)
    scale, drop = late_ref[0], late_ref[1]
    square = norm_ref[...] + scale * scale * entry(last) + drop * drop * entry(last + 2)
    square = square - 2.0 * scale * drop * entry(last + 1)
    at = last + 3
    for i in range(MATVECS):
        for j in range(i + 1):
            twice = 1.0 if i == j else 2.0
            square = square + twice * late_ref[2 + i] * late_ref[2 + j] * entry(at)
            at += 1
    scale = lax.rsqrt(jnp.maximum(square, 0.0) + EPS)

    def store(t):
        rows = pl.ds(t * ROWS, ROWS)
        return pltpu.make_async_copy(
            following_ref.at[rows, :], next_hbm.at[rows, :], store_sem.at[1 + t]
        )

    for t in range(tiles):
        @pl.loop(t * ROWS // CHUNK, (t + 1) * ROWS // CHUNK)
        def _(c):
            at = pl.ds(pl.multiple_of(c * CHUNK, CHUNK), CHUNK)
            following_ref[at, :] = (
                remain_ref[at, :] * spread(scale, CHUNK, width)
            ).astype(bf16)

        store(t).start()

    proj = proj_ref[...]
    for j in range(last):
        value = scale_ref[j] * scale_ref[last] * entry(j)
        proj = jnp.where((line == j) & (lane == last), value, proj)
    projected_ref[...] = proj[:MATVECS, :MATVECS]

    @pl.loop(0, MATVECS + 1)
    def _(r):
        sent = slots_ref.at[r, pl.ds(0, secs - 1)]
        pltpu.make_async_copy(sent, sent, sum_send.at[r]).wait()

    store_image.wait()
    for t in range(tiles):
        store(t).wait()


def finish(next_in, image_in, projected_in, next_ref, image_ref, projected_ref):
    next_ref[...] = next_in[...]
    image_ref[...] = image_in[...]
    projected_ref[...] = projected_in[...]


def per_device(
    left_env, right_env, left_block, right_block, inv_sv, precond, sector_dims, channel_charge
):
    segs, secs = lax.axis_size("seg"), lax.axis_size("sec")
    channels, width = left_env.shape[2], left_env.shape[-1]
    tiles, halves = width // ROWS, width // COLS
    halos = MATVECS * tiles * halves
    f32, bf16 = jnp.float32, jnp.bfloat16
    vmem = pl.BlockSpec(memory_space=pltpu.VMEM)
    smem = pl.BlockSpec(memory_space=pltpu.SMEM)
    hbm = pl.BlockSpec(memory_space=pl.ANY)
    out_shape = (
        jax.ShapeDtypeStruct((width, width), bf16),
        jax.ShapeDtypeStruct((width, width), f32),
        jax.ShapeDtypeStruct((MATVECS, MATVECS), f32),
    )
    dma = pltpu.SemaphoreType.DMA
    results = pl.pallas_call(
        functools.partial(kernel, segs, secs),
        name="davidson",
        out_shape=out_shape,
        in_specs=[smem, smem, hbm, hbm, hbm, hbm, vmem, hbm],
        out_specs=(hbm, hbm, vmem),
        scratch_shapes=[
            pltpu.VMEM((channels, width, width), bf16),
            pltpu.VMEM((channels, width, width), bf16),
            pltpu.VMEM((width, width), bf16),
            pltpu.VMEM((width, width), f32),
            pltpu.VMEM((width, width), bf16),
            pltpu.VMEM((1, width), bf16),
            pltpu.VMEM((width, width), bf16),
            pltpu.VMEM((MATVECS, width, width), bf16),
            pltpu.VMEM((MATVECS, ROWS, width), bf16),
            pltpu.VMEM((MATVECS, ROWS, width), bf16),
            pltpu.VMEM((ROWS, width), bf16),
            pltpu.VMEM((ROWS, width), bf16),
            pltpu.VMEM((ROWS, width), bf16),
            pltpu.VMEM((channels, width, width), bf16),
            pltpu.VMEM((channels + 1, ROWS, COLS), f32),
            pltpu.VMEM((width, width), f32),
            pltpu.VMEM((halos, ROWS, COLS), bf16),
            pltpu.VMEM((halos, ROWS, COLS), bf16),
            pltpu.VMEM((halos, ROWS, COLS), bf16),
            pltpu.VMEM((halos, ROWS, COLS), bf16),
            pltpu.VMEM((width, width), f32),
            pltpu.VMEM((width, width), f32),
            pltpu.VMEM((width, width), bf16),
            pltpu.VMEM((MATVECS + 1, secs, 1, 128), f32),
            pltpu.VMEM((8, 128), f32),
            pltpu.VMEM((MATVECS + 2, 8, 128), f32),
            pltpu.VMEM((MATVECS + 1, 8, 128), f32),
            pltpu.VMEM((MATVECS + 1, 8, 128), f32),
            pltpu.VMEM((MATVECS, 8, 128), f32),
            pltpu.VMEM((MATVECS, 8, 128), f32),
            pltpu.VMEM((8, 128), f32),
            pltpu.SMEM((channels,), jnp.int32),
            dma((4,)),
            dma((1 + halves,)),
            dma((1 + halves,)),
            dma((2,)),
            dma((2,)),
            dma((2, halos)),
            dma((2, halos)),
            dma((2, halves)),
            dma((2, halves)),
            dma((2, MATVECS)),
            dma((2, MATVECS)),
            dma((MATVECS + 1,)),
            dma((MATVECS + 1,)),
            dma((1 + tiles,)),
        ],
        compiler_params=pltpu.CompilerParams(
            collective_id=0, has_side_effects=True, vmem_limit_bytes=60 * 1024 * 1024
        ),
    )(
        channel_charge, sector_dims[0, 0], left_env[0, 0], right_env[0, 0],
        left_block[0, 0], right_block[0, 0], inv_sv[0], precond[0, 0],
    )
    following, image, projected = pl.pallas_call(
        finish, name="finish", out_shape=out_shape,
        in_specs=[vmem] * 3, out_specs=(vmem, vmem, vmem),
    )(*results)
    return following[None, None], image[None, None], projected[None]


def solution(mesh):
    in_specs = (
        P("seg", "sec", None, None, None),
        P("seg", "sec", None, None, None),
        P("seg", "sec", None, None),
        P("seg", "sec", None, None),
        P("seg", "sec", None),
        P("seg", "sec", None, None),
        P("seg", "sec", None),
        P(),
    )
    out_specs = (P("seg", "sec", None, None), P("seg", "sec", None, None), P("seg", None, None))
    return jax.shard_map(
        per_device, mesh=mesh, in_specs=in_specs, out_specs=out_specs, check_vma=False
    )
```
